32 devices in a mesh: child: 2 (over x), row: 4 (over z), col: 4 (over y, core).
Axes of the slice: x: 2, y: 2, z: 4, core: 2. Of those that a mesh axis runs over, the one named last changes fastest.
Arguments:
- contrib: float32 [2, 2048, 2048], P('child', 'row', 'col'), may hold values from -0.125 to 0.125
- assembled: float32 [2, 2048, 4096], P('child', 'row', 'col'), may hold values from -0.125 to 0.125
- pattern: int32 [16, 16], P('row', 'col'), may hold values 0 or 1
- omega: float32 [4096, 256], P('col', 'row'), may hold values from -6 to 6
- row_maps: int32 [2, 2048], P('child'), may hold values from 0 to 4095, as said below
- leaf_bounds: int32 [4], P('row'), may hold values from 448 to 576
Outputs:
- bases: float32 [4096, 256], P('row', ('child', 'col'))
- coupling: float32 [4, 2, 256, 256], P('row', None, ('child', 'col'))
The draws below stay inside these ranges and needn't reach their ends.
Inputs may be any that keep to these rules, and one draw needn't show every extreme that they name: `row_maps`: for each child, entries k * 512 to (k + 1) * 512 - 1 are distinct, rising, and lie in k * 1024 to (k + 1) * 1024 - 1.
All inputs are finite; a program needn't handle non-finite values. No bound on the sum of `pattern` on one device may be relied on, other than what follows from the above.
Results may differ from the reference program's by a relative error of at most 0.0003.
Values sent between devices are 32-bit elements; how exact they have to be, the bound alone decides.
A program may use at most 64 MiB of HBM per device.

```python
import jax
import jax.numpy as jnp
from jax import lax

TR = 512
R = 256
BT = 256
PW = 1024
FC = 2048
PF = 4096
N_ROW = 4


def draw_row_maps(key, part):
    blocks = FC // TR
    keys = jax.random.split(jax.random.fold_in(key, 17), 2 * blocks)

    def select(single_key):
        return jnp.sort(jax.random.permutation(single_key, PW)[:TR].astype(jnp.int32))
    picked = jax.vmap(select)(keys).reshape(2, blocks, TR)
    offsets = (jnp.arange(blocks, dtype=jnp.int32) * PW)[None, :, None]
    return (picked + offsets).reshape(2, FC).astype(jnp.int32)


def set_ends(array, key, least, largest):
    index_at = [jax.random.randint(jax.random.fold_in(key, axis), (), 0, length) for axis, length in enumerate(array.shape)]
    longest = array.shape.index(max(array.shape))
    next_to = index_at[:longest] + [(index_at[longest] + 1) % array.shape[longest]] + index_at[longest + 1:]
    return array.at[tuple(index_at)].set(least).at[tuple(next_to)].set(largest)


def level_of(rng, shape, cuts, least, top_value):
    gain, own = 1.0, jax.random.fold_in(rng, 6)
    for position, blocks in cuts:
        heights = jnp.exp(jax.random.uniform(jax.random.fold_in(own, position), (blocks,), jnp.float32, least / len(cuts), top_value / len(cuts)))
        gain = gain * jnp.repeat(heights, shape[position] // blocks).reshape([-1 if axis == position else 1 for axis in range(len(shape))])
    return gain


def centred(own_key, extent, deviation, most, cuts=(), kind=jnp.bfloat16):
    drawn = jax.random.normal(own_key, extent, jnp.float32) * deviation
    if len(cuts) > 0:
        drawn = level_of(own_key, extent, cuts, -0.22, 0.18) * drawn
    return jnp.clip(drawn, min=-most, max=most).astype(kind)


def setup_inputs(seed: int = 0) -> dict:
    splits = jax.random.split(jax.random.key(seed), 7)
    return {
        "contrib": centred(splits[0], (2, FC, FC), FC ** -0.5, 0.125, ((0, 2), (1, 4), (2, 4)), jnp.float32),
        "assembled": centred(splits[1], (2, PF // 2, PF), (PF // 2) ** -0.5, 0.125, ((0, 2), (1, 4), (2, 4)), jnp.float32),
        "pattern": set_ends((jax.random.randint(splits[2], (PF // BT, PF // BT), 0, 2) < 1).astype(jnp.int32), jax.random.fold_in(splits[2], 1), 0, 1),
        "omega": centred(splits[3], (PF, R), 1.0, 6.0, ((0, 4), (1, 4)), jnp.float32),
        "row_maps": draw_row_maps(jax.random.fold_in(splits[6], 71), 0),
        "leaf_bounds": set_ends(jax.random.randint(splits[5], (N_ROW,), PW // 2 - PW // 16, PW // 2 + PW // 16 + 1), jax.random.fold_in(splits[5], 1), PW // 2 - PW // 16, (PW // 2 + PW // 16 + 1) - 1).astype(jnp.int32),
    }


highest = lax.Precision.HIGHEST

def leaf_factors(window, leaf_bound):
    positions = jnp.arange(window.shape[0], dtype=jnp.int32)
    first_leaf = (positions < leaf_bound)[:, None]
    head_count = leaf_bound.astype(jnp.float32)
    tail_count = (window.shape[0] - leaf_bound).astype(jnp.float32)
    head_gram = jnp.dot(jnp.where(first_leaf, window, 0.0).T, window, precision=highest) / head_count
    tail_gram = jnp.dot(jnp.where(first_leaf, 0.0, window).T, window, precision=highest) / tail_count
    return jnp.linalg.cholesky(jnp.stack([head_gram, tail_gram]))

def leaf_bases(window, first_leaf, factors):
    head_part = lax.linalg.triangular_solve(factors[0], window, left_side=False, lower=True, transpose_a=True)
    tail_part = lax.linalg.triangular_solve(factors[1], window, left_side=False, lower=True, transpose_a=True)
    return jnp.where(first_leaf, head_part, tail_part)

def reference(contrib, assembled, pattern, omega, row_maps, leaf_bounds):
    samples = jnp.zeros((PF, R), jnp.float32)

    def window_term(window_index):
        zero_start = jnp.zeros((), jnp.int32)
        row_start = (window_index * TR).astype(jnp.int32)
        row_block = lax.dynamic_slice(assembled, (zero_start, row_start, zero_start), (2, TR, PF)).reshape(PW, PF)
        tile_start = (window_index * (PW // BT)).astype(jnp.int32)
        tiles = lax.dynamic_slice_in_dim(pattern, tile_start, PW // BT, 0).astype(jnp.float32)
        masked = (row_block.reshape(PW // BT, BT, PF // BT, BT) * tiles[:, None, :, None]).reshape(PW, PF)
        return jnp.dot(masked, omega, precision=highest)
    samples = samples + lax.map(window_term, jnp.arange(N_ROW, dtype=jnp.int32)).reshape(PF, R)
    for child_index in range(2):
        picked = jnp.take(omega, row_maps[child_index], axis=0)
        product = jnp.dot(contrib[child_index], picked, precision=highest)
        samples = samples.at[row_maps[child_index]].add(product)
    windows = samples.reshape(N_ROW, PW, R)
    factors = jax.vmap(leaf_factors)(windows, leaf_bounds)
    positions = jnp.arange(PW, dtype=jnp.int32)
    first_leaf = (positions[None, :] < leaf_bounds[:, None])[:, :, None]
    bases = jax.vmap(leaf_bases)(windows, first_leaf, factors).reshape(PF, R)
    partner = jnp.arange(N_ROW, dtype=jnp.int32) ^ 1
    sibling = jnp.take(factors, partner, axis=0)
    coupling = jnp.einsum('wlab,wlac->wlbc', factors, sibling, precision=highest)
    return (bases, coupling)
```

```python
import jax
import jax.numpy as jnp
from jax import lax
from jax.experimental import pallas as pl
from jax.experimental.pallas import tpu as pltpu
from jax.sharding import PartitionSpec as P

BT = 256
NB = 64
SUB = 8
CHUNK = 8
MESH = pl.DeviceIdType.MESH
VMEM = pl.BlockSpec(memory_space=pltpu.VMEM)
SMEM = pl.BlockSpec(memory_space=pltpu.SMEM)

NN = (((1,), (0,)), ((), ()))
NT = (((1,), (1,)), ((), ()))
TN = (((0,), (0,)), ((), ()))


def split(a):
    high = a.astype(jnp.bfloat16)
    low = (a - high.astype(jnp.float32)).astype(jnp.bfloat16)
    return high, low


def dot16(a, b, dims=NN):
    return lax.dot_general(a, b, dims, preferred_element_type=jnp.float32)


def mm3(a, b, dims=NN):
    (ah, al), (bh, bl) = split(a), split(b)
    return dot16(ah, bh, dims) + (dot16(ah, bl, dims) + dot16(al, bh, dims))


class Plane:
    def __init__(self):
        self.cols = lax.axis_size("col")
        self.chips = self.cols * lax.axis_size("child") // 2
        self.child = lax.axis_index("child")
        self.col = lax.axis_index("col")
        self.core = self.col % 2
        self.chip = (self.child * self.cols + self.col) // 2
        self.partner = {"col": self.col + 1 - 2 * self.core}
        self.across = [{"child": 1 - self.child}]
        step = 2
        while step < self.cols:
            self.across.append({"col": self.col + step - 2 * step * (self.col // step % 2)})
            step *= 2


def remote(source, target, send_sem, recv_sem, device):
    return pltpu.make_async_remote_copy(
        src_ref=source, dst_ref=target, send_sem=send_sem, recv_sem=recv_sem, device_id=device, device_id_type=MESH
    )


def greet(plane):
    count = lax.axis_size("row")
    me = lax.axis_index("row")
    barrier = pltpu.get_barrier_semaphore()

    @pl.when(me > 0)
    def _():
        pl.semaphore_signal(barrier, inc=1, device_id={"row": me - 1}, device_id_type=MESH)

    @pl.when(me < count - 1)
    def _():
        pl.semaphore_signal(barrier, inc=1, device_id={"row": me + 1}, device_id_type=MESH)

    near = [plane.partner] + plane.across
    for device in near:
        pl.semaphore_signal(barrier, inc=1, device_id=device, device_id_type=MESH)
    pl.semaphore_wait(barrier, len(near) + jnp.minimum(me, 1) + jnp.minimum(count - 1 - me, 1))


class Gather:
    def __init__(self, own_ref, out_ref, sems):
        self.own, self.out = own_ref, out_ref
        self.send_right, self.send_left, self.recv, self.swap_send, self.swap_recv, self.local_sem = sems
        self.count = lax.axis_size("row")
        self.me = lax.axis_index("row")
        self.half = lax.axis_index("child")
        self.chunks = own_ref.shape[1] // CHUNK
        self.has_left = self.me > 0
        self.has_right = self.me < self.count - 1

    def rows(self, chunk):
        return slice(chunk * CHUNK, (chunk + 1) * CHUNK)

    def hop(self, block, target, step, send, chunk):
        place = self.out.at[block, self.half, self.rows(chunk)]
        source = self.own.at[self.half, self.rows(chunk)] if step == 0 else place
        return remote(source, place, send.at[block, chunk], self.recv.at[block, chunk], {"row": target})

    def swap(self, block, chunk, half):
        place = self.out.at[block, half, self.rows(chunk)]
        sems = (self.swap_send.at[block, chunk], self.swap_recv.at[block, chunk])
        return remote(place, place, *sems, {"child": 1 - self.half})

    def pass_on(self, step, chunk):
        low, high = self.me - step, self.me + step
        if step > 0:

            @pl.when(low >= 0)
            def _():
                self.hop(low, self.me - 1, step, self.send_right, chunk).wait_recv()

        @pl.when(jnp.logical_and(low >= 0, self.has_right))
        def _():
            self.hop(low, self.me + 1, step, self.send_right, chunk).start()

        if step > 0:

            @pl.when(low >= 0)
            def _():
                self.swap(low, chunk, self.half).start()

            @pl.when(high < self.count)
            def _():
                self.hop(high, self.me + 1, step, self.send_left, chunk).wait_recv()

        @pl.when(jnp.logical_and(high < self.count, self.has_left))
        def _():
            self.hop(high, self.me - 1, step, self.send_left, chunk).start()

        if step > 0:

            @pl.when(high < self.count)
            def _():
                self.swap(high, chunk, self.half).start()

    def run(self, work):
        keep = pltpu.make_async_copy(self.own, self.out.at[self.me], self.local_sem)
        keep.start()
        for step in range(self.count):
            for chunk in range(self.chunks):
                self.pass_on(step, chunk)
                if step == 0 and chunk == self.chunks - 1:
                    keep.wait()
                for act in work.get((step, chunk), ()):
                    act()

    def nth(self, n):
        left, right = self.me, self.count - 1 - self.me
        both = jnp.minimum(left, right)
        near = (n + 1) // 2
        beside = self.me - near if n % 2 == 1 else self.me + near
        beyond = jnp.where(left < right, self.me + n - both, self.me - n + both)
        return jnp.where(n <= 2 * both, beside, beyond)

    def arrive(self, block):
        for chunk in range(self.chunks):
            self.swap(block, chunk, 1 - self.half).wait_recv()

    def drain(self):
        for step in range(self.count):
            low, high = self.me - step, self.me + step
            for chunk in range(self.chunks):

                @pl.when(jnp.logical_and(low >= 0, self.has_right))
                def _():
                    self.hop(low, self.me + 1, step, self.send_right, chunk).wait_send()

                @pl.when(jnp.logical_and(high < self.count, self.has_left))
                def _():
                    self.hop(high, self.me - 1, step, self.send_left, chunk).wait_send()

        for step in range(1, self.count):
            for chunk in range(self.chunks):
                self.swap(lax.rem(self.me + step, self.count), chunk, self.half).wait_send()


def prepare_sketch(pattern_ref, contrib, assembled, maps_ref, held):
    pick, place, front, entries = held
    half = lax.axis_index("child")
    tile_rows, tile_cols = contrib.shape
    window_rows = assembled.shape[1]
    row_pos, col_pos = lax.axis_index("row"), lax.axis_index("col")
    columns = maps_ref[:, pl.ds(pl.multiple_of(col_pos * tile_cols, tile_cols), tile_cols)] - col_pos * window_rows
    targets = maps_ref[:, pl.ds(pl.multiple_of(row_pos * tile_rows, tile_rows), tile_rows)] - row_pos * window_rows
    index = lax.broadcasted_iota(jnp.int32, (window_rows, tile_cols), 0)
    pick[...] = jnp.where(index == columns, 1.0, 0.0).astype(jnp.bfloat16)
    index = lax.broadcasted_iota(jnp.int32, (window_rows, tile_rows), 0)
    place[...] = jnp.where(index == targets, 1.0, 0.0).astype(jnp.bfloat16)
    front[0], front[1] = split(contrib[...])
    for row in range(tile_rows // BT):
        for col in range(window_rows // BT):
            where = (slice(row * BT, (row + 1) * BT), slice(col * BT, (col + 1) * BT))
            present = pattern_ref[half * (tile_rows // BT) + row, col].astype(jnp.float32)
            entries[(0,) + where], entries[(1,) + where] = split(assembled[where] * present)


def stacked(a, b, dims=NN):
    rows = a.shape[0] // 2
    both = dot16(a, b[0], dims)
    return both[:rows] + (dot16(a[:rows], b[1], dims) + both[rows:])


def sketch(omega, held, part_ref):
    pick, place, front, entries = held
    half = lax.axis_index("child")
    rows, tile_rows = omega.shape[0], place.shape[1]
    both = jnp.concatenate(split(omega), axis=0)
    picked = dot16(both, pick[...]).astype(jnp.bfloat16)
    product = stacked(picked, front, NT)
    sparse = stacked(both, entries, NT)
    spread = dot16(jnp.concatenate(split(product), axis=0), place[...], NT)
    part_ref[...] = spread[:rows] + spread[rows:]
    where = pl.ds(pl.multiple_of(half * tile_rows, tile_rows), tile_rows)
    part_ref[:, where] = part_ref[:, where] + sparse


class Total:
    def __init__(self, plane, part, sums, pair_buf, landed, window, offsets, sems):
        self.plane, self.part, self.sums, self.pair_buf = plane, part, sums, pair_buf
        self.landed, self.window = landed, window
        self.own, self.other = offsets
        self.pair_send, self.pair_recv, self.send, self.recv = sems
        self.phases = len(plane.across)

    def lanes(self, offset):
        return pl.ds(pl.multiple_of(offset, 128), self.window.shape[2])

    def pair(self, r):
        source = self.part.at[r, :, self.lanes(self.other)]
        return remote(source, self.pair_buf.at[r], self.pair_send.at[r], self.pair_recv.at[r], self.plane.partner)

    def cross(self, r, phase, side):
        half = self.window.shape[1] // 2
        rows = slice(side * half, (side + 1) * half)
        device = self.plane.across[(phase + side) % self.phases]
        sems = (self.send.at[r, phase, side], self.recv.at[r, phase, side])
        return remote(self.sums.at[r, phase, rows], self.landed.at[r, phase, rows], *sems, device), rows

    def begin(self, r):
        self.pair(r).start()

    def advance(self, r, phase):
        if phase == 0:
            self.pair(r).wait_recv()
            self.sums[r, 0] = self.part[r, :, self.lanes(self.own)] + self.pair_buf[r]
            for side in range(2):
                self.cross(r, 0, side)[0].start()
            return
        for side in range(2):
            copy, rows = self.cross(r, phase - 1, side)
            copy.wait_recv()
            total = self.sums[r, phase - 1, rows] + self.landed[r, phase - 1, rows]
            if phase < self.phases:
                self.sums[r, phase, rows] = total
                self.cross(r, phase, side)[0].start()
            else:
                self.window[r, rows] = total

    def drain(self, stages):
        for r in range(stages):
            self.pair(r).wait_send()
            for phase in range(self.phases):
                for side in range(2):
                    self.cross(r, phase, side)[0].wait_send()


def eliminate(leaves):
    groups = NB // SUB
    index = lax.broadcasted_iota(jnp.int32, (SUB, 2 * NB), 0)
    wide = (SUB, 2 * NB)
    leaves = [list(rows) for rows in leaves]
    for panel in range(groups):
        first = panel * SUB
        columns = [
            {
                q: [jnp.broadcast_to(rows[q][:, first + k : first + k + 1], wide) for k in range(SUB)]
                for q in range(panel, groups)
            }
            for rows in leaves
        ]
        for k in range(SUB):
            for rows, cols in zip(leaves, columns):
                own = cols[panel]
                scale = lax.rsqrt(jnp.broadcast_to(own[k][k : k + 1], wide))
                pivot = jnp.broadcast_to(rows[panel][k : k + 1], wide) * scale
                weight = {q: cols[q][k] * scale for q in range(panel, groups)}
                across = weight[panel]
                below = jnp.where(index > k, across, 0.0)
                rows[panel] = jnp.where(index == k, pivot, rows[panel] - below * pivot)
                for j in range(k + 1, SUB):
                    factor = jnp.broadcast_to(across[j : j + 1], wide)
                    for q in range(panel, groups):
                        cols[q][j] = cols[q][j] - (below if q == panel else weight[q]) * factor
                for q in range(panel + 1, groups):
                    rows[q] = rows[q] - weight[q] * pivot
    return leaves


def factor(gram, work, done_block):
    columns = gram.shape[0]
    eye = jnp.where(
        lax.broadcasted_iota(jnp.int32, (columns, columns), 0)
        == lax.broadcasted_iota(jnp.int32, (columns, columns), 1),
        1.0,
        0.0,
    )
    work[:, :columns] = gram
    work[:, columns:] = eye
    small_eye = eye[:NB, :NB]
    for block in range(columns // NB):
        begin, end = block * NB, (block + 1) * NB
        diagonal = jnp.concatenate([work[begin:end, begin:end], small_eye], axis=1)
        done = eliminate([[diagonal[q * SUB : (q + 1) * SUB] for q in range(NB // SUB)]])
        inverse = jnp.concatenate(done[0], axis=0)[:, NB:]
        rows = mm3(inverse, work[begin:end, :])
        work[begin:end, :] = rows
        done_block(block, begin, end, rows[:, :columns])
        if end < columns:
            work[end:, :] = work[end:, :] - mm3(rows[:, end:columns], rows, TN)


def whole_kernel(
    bound_ref, pattern_ref, omega_ref, contrib_ref, assembled_ref, maps_ref, bases_ref, coupling_ref,
    gathered, contrib_buf, assembled_buf, pick, place, front, entries,
    part, sums, pair_buf, landed, window, work, upper, sibling, bases_out, bases_in, coupling_out, coupling_in,
    input_sems, *sems,
):
    plane = Plane()
    core = plane.core
    window_rows = assembled_buf.shape[1]
    columns, width = upper.shape[1], bases_ref.shape[0]
    stages, span = window.shape[0], window.shape[2]
    low = window_rows - span
    held = (pick, place, front, entries)
    load_front = pltpu.make_async_copy(contrib_ref.at[0], contrib_buf, input_sems.at[0])
    load_entries = pltpu.make_async_copy(assembled_ref.at[0], assembled_buf, input_sems.at[1])
    load_front.start()
    load_entries.start()
    greet(plane)

    row_count, row_pos = lax.axis_size("row"), lax.axis_index("row")
    gather = Gather(omega_ref, gathered, sems[:6])
    summing = Total(plane, part, sums, pair_buf, landed, window, (core * low, (1 - core) * low), sems[6:10])
    last = len(plane.across)

    def prepare():
        load_front.wait()
        load_entries.wait()
        prepare_sketch(pattern_ref, contrib_buf, assembled_buf, maps_ref, held)

    def stage(n):
        block = row_pos if n == 0 else gather.nth(n)
        if n > 0:
            gather.arrive(block)
        sketch(gathered[block].reshape(columns // stages, window_rows), held, part.at[block])
        summing.begin(block)

    def advance(n, phase):
        summing.advance(row_pos if n == 0 else gather.nth(n), phase)

    if stages == row_count:
        chunks = gather.chunks
        waiting = [(n, phase) for n in range(stages - 2) for phase in range(last + 1)]
        work_at = {(0, chunks - 1): [prepare, lambda: stage(0)]}
        taken = []

        def put(step, chunk, act, key):
            work_at.setdefault((min(step, row_count - 1), min(chunk, chunks - 1)), []).append(act)
            taken.append(key)

        put(1, chunks // 2, lambda: advance(0, 0), (0, 0))
        put(2, chunks - 1, lambda: advance(0, 1), (0, 1))
        first = None
        if stages > 2:
            put(3, 0, lambda: stage(1), "stage 1")
            put(3, chunks // 2, lambda: advance(1, 0), (1, 0))
        gather.run(work_at)
        pending = {n: [p for p in range(last + 1) if (n, p) not in taken] for n in range(stages)}
        started = [0] + ([1] if stages > 2 else [])

        def go():
            for n in started:
                if pending[n]:
                    phase = pending[n].pop(0)
                    advance(n, phase)

        for n in range(stages):
            if n in started:
                continue
            stage(n)
            started.append(n)
            go()
        while any(pending.values()):
            go()
    else:
        gather.run({(0, 0): [prepare]})
        for step in range(1, row_count):
            gather.arrive(lax.rem(row_pos + step, row_count))
        sketch(gathered[...].reshape(columns, window_rows), held, part.at[0])
        summing.begin(0)
        for phase in range(last + 1):
            summing.advance(0, phase)

    near_send, near_recv, end_send, end_recv = sems[10:]
    near = {"row": row_pos + 1 - 2 * (row_pos % 2)}

    def send(block):
        start = block * NB // 128 * 128
        rows = slice(block * NB, (block + 1) * NB)
        source, target = upper.at[rows, start:], sibling.at[rows, start:]
        return remote(source, target, near_send.at[block], near_recv.at[block], near)

    def done_block(block, begin, end, rows):
        keep = lax.broadcasted_iota(jnp.int32, rows.shape, 1) >= begin + lax.broadcasted_iota(
            jnp.int32, rows.shape, 0
        )
        upper[begin:end, :] = jnp.where(keep, rows, 0.0)
        send(block).start()

    bound = bound_ref[0]
    samples = window[...].reshape(columns, span)
    place_of = lax.broadcasted_iota(jnp.int32, (columns, span), 1) + core * low
    masked = jnp.where((1 - 2 * core) * (bound - place_of) + core > 0, samples, 0.0)
    rows_of_leaf = (1 - core) * bound + core * (window_rows - bound)
    factor(mm3(masked, masked, NT) / rows_of_leaf.astype(jnp.float32), work, done_block)

    pair_rows = pl.ds(pl.multiple_of(plane.chip * 2 * width, 2 * width), 2 * width)
    give_bases = remote(
        bases_out.at[1 - core], bases_in.at[core], end_send.at[0], end_recv.at[0], plane.partner
    )
    give_coupling = remote(
        coupling_out.at[1 - core], coupling_in.at[core], end_send.at[1], end_recv.at[1], plane.partner
    )
    bases_out[...] = mm3(work[pair_rows, columns:], samples).reshape(bases_out.shape)
    give_bases.start()
    own = upper[pair_rows, :]
    for block in range(columns // NB):
        start = block * NB // 128 * 128
        send(block).wait_recv()
        piece = mm3(own[:, start:], sibling[block * NB : (block + 1) * NB, start:], NT)
        coupling_out[:, :, block * NB : (block + 1) * NB] = piece.reshape(2, width, NB)
    give_coupling.start()
    bases_in[core] = bases_out[core]
    coupling_ref[0, core] = coupling_out[core]
    remote(
        bases_out.at[core], bases_in.at[1 - core], end_send.at[0], end_recv.at[0], plane.partner
    ).wait_recv()
    bases_ref[:, :low] = bases_in[0, :, :low]
    bases_ref[:, span:] = bases_in[1, :, span - low :]
    lane = lax.broadcasted_iota(jnp.int32, (width, span - low), 1) + low
    bases_ref[:, low:span] = jnp.where(lane < bound, bases_in[0, :, low:], bases_in[1, :, : span - low])
    remote(
        coupling_out.at[core], coupling_in.at[1 - core], end_send.at[1], end_recv.at[1], plane.partner
    ).wait_recv()
    coupling_ref[0, 1 - core] = coupling_in[1 - core]

    gather.drain()
    summing.drain(stages)
    for block in range(columns // NB):
        send(block).wait_send()
    give_bases.wait_send()
    give_coupling.wait_send()


def deliver_kernel(bases_ref, coupling_ref, bases_out, coupling_out):
    bases_out[...] = bases_ref[...]
    coupling_out[...] = coupling_ref[...]


def local(contrib, assembled, pattern, omega, row_maps, leaf_bounds):
    tile_rows, tile_cols = contrib.shape[1:]
    window_rows, own_width = omega.shape
    rows = lax.axis_size("row")
    cols = lax.axis_size("col")
    chips = cols * lax.axis_size("child") // 2
    columns = own_width * rows
    width = columns // (2 * chips)
    phases = 1 + (cols // 2).bit_length() - 1
    span = (window_rows // 2 + window_rows // 16 + 127) // 128 * 128
    own = omega.T.reshape(2, own_width // 2, window_rows)
    f32, bf16, dma = jnp.float32, jnp.bfloat16, pltpu.SemaphoreType.DMA
    any_space = pl.BlockSpec(memory_space=pl.ANY)
    stages = rows if own_width >= 8 * SUB else 1
    depth = columns // stages
    chunks = own_width // 2 // CHUNK
    bases, coupling = pl.pallas_call(
        whole_kernel,
        out_shape=(
            jax.ShapeDtypeStruct((width, window_rows), f32),
            jax.ShapeDtypeStruct((1, 2, width, columns), f32),
        ),
        in_specs=[SMEM, SMEM, VMEM, any_space, any_space, VMEM],
        out_specs=(VMEM, VMEM),
        scratch_shapes=[
            pltpu.VMEM((rows, 2, own_width // 2, window_rows), f32),
            pltpu.VMEM((tile_rows, tile_cols), f32),
            pltpu.VMEM((tile_rows, window_rows), f32),
            pltpu.VMEM((window_rows, tile_cols), bf16),
            pltpu.VMEM((window_rows, tile_rows), bf16),
            pltpu.VMEM((2, tile_rows, tile_cols), bf16),
            pltpu.VMEM((2, tile_rows, window_rows), bf16),
            pltpu.VMEM((stages, depth, window_rows), f32),
            pltpu.VMEM((stages, phases, depth, span), f32),
            pltpu.VMEM((stages, depth, span), f32),
            pltpu.VMEM((stages, phases, depth, span), f32),
            pltpu.VMEM((stages, depth, span), f32),
            pltpu.VMEM((columns, 2 * columns), f32),
            pltpu.VMEM((columns, columns), f32),
            pltpu.VMEM((columns, columns), f32),
            pltpu.VMEM((2, width, span), f32),
            pltpu.VMEM((2, width, span), f32),
            pltpu.VMEM((2, width, columns), f32),
            pltpu.VMEM((2, width, columns), f32),
            dma((2,)),
        ]
        + [dma((rows, chunks))] * 5
        + [dma]
        + [dma((stages,))] * 2
        + [dma((stages, phases, 2))] * 2
        + [dma((columns // NB,))] * 2
        + [dma((2,))] * 2,
        compiler_params=pltpu.CompilerParams(
            collective_id=0, has_side_effects=True, vmem_limit_bytes=56 << 20
        ),
        name="front_samples",
    )(leaf_bounds, pattern, own, contrib, assembled, row_maps)
    bases, coupling = pl.pallas_call(
        deliver_kernel,
        out_shape=(
            jax.ShapeDtypeStruct(bases.shape, f32),
            jax.ShapeDtypeStruct(coupling.shape, f32),
        ),
        in_specs=[VMEM, VMEM],
        out_specs=(VMEM, VMEM),
        name="deliver",
    )(bases, coupling)
    return (bases.T, coupling)


def solution(mesh):
    in_specs = (
        P("child", "row", "col"),
        P("child", "row", "col"),
        P("row", "col"),
        P("col", "row"),
        P("child", None),
        P("row"),
    )
    out_specs = (P("row", ("child", "col")), P("row", None, ("child", "col"), None))
    return jax.shard_map(local, mesh=mesh, in_specs=in_specs, out_specs=out_specs, check_vma=False)
```

```python
import jax
import jax.numpy as jnp
from jax import lax
from jax.experimental import pallas as pl
from jax.experimental.pallas import tpu as pltpu
from jax.sharding import PartitionSpec as P

BT = 256
NB = 64
SUB = 8
CHUNK = 8
ROOM = 8 << 20
SMALL = 62 << 20
DOUBLED = 1
MESH = pl.DeviceIdType.MESH
VMEM = pl.BlockSpec(memory_space=pltpu.VMEM)
SMEM = pl.BlockSpec(memory_space=pltpu.SMEM)

NN = (((1,), (0,)), ((), ()))
NT = (((1,), (1,)), ((), ()))
TN = (((0,), (0,)), ((), ()))


def split(a):
    high = a.astype(jnp.bfloat16)
    low = (a - high.astype(jnp.float32)).astype(jnp.bfloat16)
    return high, low


def dot16(a, b, dims=NN):
    return lax.dot_general(a, b, dims, preferred_element_type=jnp.float32)


def mm3(a, b, dims=NN):
    (ah, al), (bh, bl) = split(a), split(b)
    return dot16(ah, bh, dims) + (dot16(ah, bl, dims) + dot16(al, bh, dims))


class Plane:
    def __init__(self):
        self.cols = lax.axis_size("col")
        self.chips = self.cols * lax.axis_size("child") // 2
        self.child = lax.axis_index("child")
        self.col = lax.axis_index("col")
        self.core = self.col % 2
        self.chip = (self.child * self.cols + self.col) // 2
        self.partner = {"col": self.col + 1 - 2 * self.core}
        self.across = [{"child": 1 - self.child}]
        step = 2
        while step < self.cols:
            self.across.append({"col": self.col + step - 2 * step * (self.col // step % 2)})
            step *= 2
        self.high = self.col // 2 % 2


def remote(source, target, send_sem, recv_sem, device):
    return pltpu.make_async_remote_copy(
        src_ref=source, dst_ref=target, send_sem=send_sem, recv_sem=recv_sem, device_id=device, device_id_type=MESH
    )


def greet(plane):
    count = lax.axis_size("row")
    me = lax.axis_index("row")
    barrier = pltpu.get_barrier_semaphore()

    @pl.when(me > 0)
    def _():
        pl.semaphore_signal(barrier, inc=1, device_id={"row": me - 1}, device_id_type=MESH)

    @pl.when(me < count - 1)
    def _():
        pl.semaphore_signal(barrier, inc=1, device_id={"row": me + 1}, device_id_type=MESH)

    near = [plane.partner] + plane.across
    for device in near:
        pl.semaphore_signal(barrier, inc=1, device_id=device, device_id_type=MESH)
    pl.semaphore_wait(barrier, len(near) + jnp.minimum(me, 1) + jnp.minimum(count - 1 - me, 1))


class Gather:
    def __init__(self, own_ref, out_ref, sems):
        self.own, self.out = own_ref, out_ref
        self.send_right, self.send_left, self.recv, self.swap_send, self.swap_recv, self.local_sem = sems
        self.count = lax.axis_size("row")
        self.me = lax.axis_index("row")
        self.half = lax.axis_index("child")
        self.chunks = own_ref.shape[1] // CHUNK
        self.has_left = self.me > 0
        self.has_right = self.me < self.count - 1

    def rows(self, chunk):
        return slice(chunk * CHUNK, (chunk + 1) * CHUNK)

    def hop(self, block, target, step, send, chunk):
        place = self.out.at[block, self.half, self.rows(chunk)]
        source = self.own.at[self.half, self.rows(chunk)] if step == 0 else place
        return remote(source, place, send.at[block, chunk], self.recv.at[block, chunk], {"row": target})

    def swap(self, block, chunk, half):
        place = self.out.at[block, half, self.rows(chunk)]
        sems = (self.swap_send.at[block, chunk], self.swap_recv.at[block, chunk])
        return remote(place, place, *sems, {"child": 1 - self.half})

    def pass_on(self, step, chunk):
        low, high = self.me - step, self.me + step
        if step > 0:

            @pl.when(low >= 0)
            def _():
                self.hop(low, self.me - 1, step, self.send_right, chunk).wait_recv()

        @pl.when(jnp.logical_and(low >= 0, self.has_right))
        def _():
            self.hop(low, self.me + 1, step, self.send_right, chunk).start()

        if step > 0:

            @pl.when(low >= 0)
            def _():
                self.swap(low, chunk, self.half).start()

            @pl.when(high < self.count)
            def _():
                self.hop(high, self.me + 1, step, self.send_left, chunk).wait_recv()

        @pl.when(jnp.logical_and(high < self.count, self.has_left))
        def _():
            self.hop(high, self.me - 1, step, self.send_left, chunk).start()

        if step > 0:

            @pl.when(high < self.count)
            def _():
                self.swap(high, chunk, self.half).start()

    def run(self, work):
        keep = pltpu.make_async_copy(self.own, self.out.at[self.me], self.local_sem)
        keep.start()
        for step in range(self.count):
            for chunk in range(self.chunks):
                self.pass_on(step, chunk)
                if step == 0 and chunk == self.chunks - 1:
                    keep.wait()
                for act in work.get((step, chunk), ()):
                    act()

    def nth(self, n):
        left, right = self.me, self.count - 1 - self.me
        both = jnp.minimum(left, right)
        near = (n + 1) // 2
        beside = self.me - near if n % 2 == 1 else self.me + near
        beyond = jnp.where(left < right, self.me + n - both, self.me - n + both)
        return jnp.where(n <= 2 * both, beside, beyond)

    def arrive(self, block):
        for chunk in range(self.chunks):
            self.swap(block, chunk, 1 - self.half).wait_recv()

    def drain(self):
        for step in range(self.count):
            low, high = self.me - step, self.me + step
            for chunk in range(self.chunks):

                @pl.when(jnp.logical_and(low >= 0, self.has_right))
                def _():
                    self.hop(low, self.me + 1, step, self.send_right, chunk).wait_send()

                @pl.when(jnp.logical_and(high < self.count, self.has_left))
                def _():
                    self.hop(high, self.me - 1, step, self.send_left, chunk).wait_send()

        for step in range(1, self.count):
            for chunk in range(self.chunks):
                self.swap(lax.rem(self.me + step, self.count), chunk, self.half).wait_send()


def prepare_sketch(pattern_ref, contrib, assembled, maps_ref, held):
    pick, place, front, entries = held
    half = lax.axis_index("child")
    tile_rows, tile_cols = contrib.shape
    window_rows = assembled.shape[1]
    row_pos, col_pos = lax.axis_index("row"), lax.axis_index("col")
    columns = maps_ref[:, pl.ds(pl.multiple_of(col_pos * tile_cols, tile_cols), tile_cols)] - col_pos * window_rows
    targets = maps_ref[:, pl.ds(pl.multiple_of(row_pos * tile_rows, tile_rows), tile_rows)] - row_pos * window_rows
    index = lax.broadcasted_iota(jnp.int32, (window_rows, tile_cols), 0)
    pick[...] = jnp.where(index == columns, 1.0, 0.0).astype(jnp.bfloat16)
    index = lax.broadcasted_iota(jnp.int32, (window_rows, tile_rows), 0)
    place[...] = jnp.where(index == targets, 1.0, 0.0).astype(jnp.bfloat16)
    front[0], front[1] = split(contrib[...])
    for row in range(tile_rows // BT):
        for col in range(window_rows // BT):
            where = (slice(row * BT, (row + 1) * BT), slice(col * BT, (col + 1) * BT))
            present = pattern_ref[half * (tile_rows // BT) + row, col].astype(jnp.float32)
            entries[(0,) + where], entries[(1,) + where] = split(assembled[where] * present)


def stacked(a, b, dims=NN):
    rows = a.shape[0] // 2
    both = dot16(a, b[0], dims)
    return both[:rows] + (dot16(a[:rows], b[1], dims) + both[rows:])


def sketch(omega, held, part_ref):
    pick, place, front, entries = held
    half = lax.axis_index("child")
    rows, tile_rows = omega.shape[0], place.shape[1]
    both = jnp.concatenate(split(omega), axis=0)
    picked = dot16(both, pick[...]).astype(jnp.bfloat16)
    product = stacked(picked, front, NT)
    sparse = stacked(both, entries, NT)
    spread = dot16(jnp.concatenate(split(product), axis=0), place[...], NT)
    part_ref[...] = spread[:rows] + spread[rows:]
    where = pl.ds(pl.multiple_of(half * tile_rows, tile_rows), tile_rows)
    part_ref[:, where] = part_ref[:, where] + sparse


class Total:
    def __init__(self, plane, part, sums, pair_buf, landed, window, sems):
        self.plane, self.part, self.sums, self.pair_buf = plane, part, sums, pair_buf
        self.landed, self.window = landed, window
        self.pair_send, self.pair_recv, self.send, self.recv, self.hand_send, self.hand_recv = sems
        self.phases = len(plane.across)
        self.depth, self.half = pair_buf.shape[1:]
        self.shared = window.shape[2] - self.half
        self.place = self.lanes(plane.core * self.shared, self.half)

    def lanes(self, offset, size):
        return pl.ds(pl.multiple_of(offset, 128), size)

    def side(self, which):
        return pl.ds(pl.multiple_of(which * (self.depth // 2), SUB), self.depth // 2)

    def pair(self, r):
        source = self.part.at[r, :, self.lanes((1 - self.plane.core) * self.half, self.half)]
        return remote(source, self.pair_buf.at[r], self.pair_send.at[r], self.pair_recv.at[r], self.plane.partner)

    def hand(self, r):
        core, half, shared = self.plane.core, self.half, self.shared
        source = self.window.at[r, :, self.lanes((1 - core) * (half - shared) + core * shared, shared)]
        target = self.window.at[r, :, self.lanes(core * half, shared)]
        return remote(source, target, self.hand_send.at[r], self.hand_recv.at[r], self.plane.partner)

    def cross(self, r, phase, side):
        device = self.plane.across[(phase + side) % self.phases]
        rows = self.side(side)
        sems = (self.send.at[r, phase, side], self.recv.at[r, phase, side])
        return remote(self.sums.at[r, phase, rows], self.landed.at[r, phase, rows], *sems, device)

    def scatter(self, r, phase, arriving=False):
        keep, away = self.plane.high, 1 - self.plane.high
        sems = (self.send.at[r, phase, 0], self.recv.at[r, phase, 0])
        if phase == 0:
            rows = self.side(keep if arriving else away)
            return remote(self.sums.at[r, 0, rows], self.landed.at[r, 0, rows], *sems, self.plane.across[1])
        if phase == 1:
            rows = self.side(keep)
            return remote(self.sums.at[r, 1, rows], self.landed.at[r, 1, rows], *sems, self.plane.across[0])
        place = self.window.at[r, self.side(away if arriving else keep), self.place]
        return remote(place, place, *sems, self.plane.across[1])

    def begin(self, r):
        self.pair(r).start()

    def steps(self, double):
        return self.phases + 1 if double else 4

    def advance(self, r, phase, double):
        if phase == 0:
            self.pair(r).wait_recv()
            own = self.lanes(self.plane.core * self.half, self.half)
            self.sums[r, 0] = self.part[r, :, own] + self.pair_buf[r]
            if double:
                for side in range(2):
                    self.cross(r, 0, side).start()
            else:
                self.scatter(r, 0).start()
            return
        if double:
            for side in range(2):
                rows = self.side(side)
                self.cross(r, phase - 1, side).wait_recv()
                total = self.sums[r, phase - 1, rows] + self.landed[r, phase - 1, rows]
                if phase < self.phases:
                    self.sums[r, phase, rows] = total
                    self.cross(r, phase, side).start()
                else:
                    self.window[r, rows, self.place] = total
            if phase == self.phases:
                self.hand(r).start()
            return
        self.scatter(r, phase - 1, True).wait_recv()
        if phase == 3:
            self.hand(r).start()
            return
        rows = self.side(self.plane.high)
        total = self.sums[r, phase - 1, rows] + self.landed[r, phase - 1, rows]
        if phase == 1:
            self.sums[r, 1, rows] = total
        else:
            self.window[r, rows, self.place] = total
        self.scatter(r, phase).start()

    def arrive(self, r):
        core, half, shared = self.plane.core, self.half, self.shared
        target = self.window.at[r, :, self.lanes((1 - core) * half, shared)]
        remote(target, target, self.hand_send.at[r], self.hand_recv.at[r], self.plane.partner).wait_recv()

    def drain(self, r, double):
        self.pair(r).wait_send()
        self.hand(r).wait_send()
        if double:
            for phase in range(self.phases):
                for side in range(2):
                    self.cross(r, phase, side).wait_send()
        else:
            for phase in range(3):
                self.scatter(r, phase).wait_send()


def eliminate(leaves):
    groups = NB // SUB
    index = lax.broadcasted_iota(jnp.int32, (SUB, 2 * NB), 0)
    wide = (SUB, 2 * NB)
    leaves = [list(rows) for rows in leaves]
    for panel in range(groups):
        first = panel * SUB
        columns = [
            {
                q: [jnp.broadcast_to(rows[q][:, first + k : first + k + 1], wide) for k in range(SUB)]
                for q in range(panel, groups)
            }
            for rows in leaves
        ]
        for k in range(SUB):
            for rows, cols in zip(leaves, columns):
                own = cols[panel]
                scale = lax.rsqrt(jnp.broadcast_to(own[k][k : k + 1], wide))
                pivot = jnp.broadcast_to(rows[panel][k : k + 1], wide) * scale
                weight = {q: cols[q][k] * scale for q in range(panel, groups)}
                across = weight[panel]
                below = jnp.where(index > k, across, 0.0)
                rows[panel] = jnp.where(index == k, pivot, rows[panel] - below * pivot)
                for j in range(k + 1, SUB):
                    factor = jnp.broadcast_to(across[j : j + 1], wide)
                    for q in range(panel, groups):
                        cols[q][j] = cols[q][j] - (below if q == panel else weight[q]) * factor
                for q in range(panel + 1, groups):
                    rows[q] = rows[q] - weight[q] * pivot
    return leaves


def factor(gram, work, done_block):
    columns = gram.shape[0]
    eye = jnp.where(
        lax.broadcasted_iota(jnp.int32, (columns, columns), 0)
        == lax.broadcasted_iota(jnp.int32, (columns, columns), 1),
        1.0,
        0.0,
    )
    work[:, :columns] = gram
    work[:, columns:] = eye
    small_eye = eye[:NB, :NB]
    for block in range(columns // NB):
        begin, end = block * NB, (block + 1) * NB
        diagonal = jnp.concatenate([work[begin:end, begin:end], small_eye], axis=1)
        done = eliminate([[diagonal[q * SUB : (q + 1) * SUB] for q in range(NB // SUB)]])
        inverse = jnp.concatenate(done[0], axis=0)[:, NB:]
        rows = mm3(inverse, work[begin:end, :])
        work[begin:end, :] = rows
        done_block(block, begin, end, rows[:, :columns])
        if end < columns:
            work[end:, :] = work[end:, :] - mm3(rows[:, end:columns], rows, TN)


def whole_kernel(
    bound_ref, pattern_hbm, omega_ref, contrib_ref, assembled_ref, maps_hbm, bases_ref, coupling_ref,
    pattern_ref, maps_ref, gathered, contrib_buf, assembled_buf, pick, place, front, entries,
    part, sums, pair_buf, landed, window, work, upper, sibling, bases_out, bases_in, coupling_out, coupling_in,
    input_sems, *sems,
):
    plane = Plane()
    core = plane.core
    window_rows = assembled_buf.shape[1]
    columns, width = upper.shape[1], bases_ref.shape[0]
    stages, span = window.shape[0], window.shape[2]
    low = window_rows - span
    held = (pick, place, front, entries)
    load_front = pltpu.make_async_copy(contrib_ref.at[0], contrib_buf, input_sems.at[0])
    load_entries = pltpu.make_async_copy(assembled_ref.at[0], assembled_buf, input_sems.at[1])
    load_small = [
        pltpu.make_async_copy(source, target, input_sems.at[2 + i])
        for i, (source, target) in enumerate(
            ((maps_hbm, maps_ref), (pattern_hbm, pattern_ref))
        )
    ]
    for copy in load_small + [load_front, load_entries]:
        copy.start()
    greet(plane)

    row_count, row_pos = lax.axis_size("row"), lax.axis_index("row")
    gather = Gather(omega_ref, gathered, sems[:6])
    summing = Total(plane, part, sums, pair_buf, landed, window, sems[6:12])

    def prepare():
        for copy in load_small + [load_front, load_entries]:
            copy.wait()
        prepare_sketch(pattern_ref, contrib_buf, assembled_buf, maps_ref, held)

    def block_of(n):
        return row_pos if n == 0 else gather.nth(n)

    def double(n):
        return n >= stages - DOUBLED

    def stage(n):
        block = block_of(n)
        if n > 0:
            gather.arrive(block)
        sketch(gathered[block].reshape(columns // stages, window_rows), held, part.at[block])
        summing.begin(block)

    if stages == row_count:
        begun, left = [], {}

        def begin(n):
            stage(n)
            begun.append(n)
            left[n] = list(range(summing.steps(double(n))))

        def go(n):
            if n in left and left[n]:
                summing.advance(block_of(n), left[n].pop(0), double(n))

        def go_all():
            for n in list(begun):
                go(n)

        end, mid = gather.chunks - 1, gather.chunks // 2
        queue = {(0, end): [prepare, lambda: begin(0)]}
        queue.setdefault((1, mid), []).append(lambda: go(0))
        queue.setdefault((2, end), []).append(lambda: go(0))
        if row_count > 3:
            queue.setdefault((3, 0), []).append(lambda: begin(1))
        gather.run(queue)
        go(1)
        for n in range(len(begun), stages):
            begin(n)
            go_all()
        while any(left.values()):
            go_all()
        blocks = range(stages)
        for n in blocks:
            summing.arrive(block_of(n))
    else:
        gather.run({(0, 0): [prepare]})
        for step in range(1, row_count):
            gather.arrive(lax.rem(row_pos + step, row_count))
        sketch(gathered[...].reshape(columns, window_rows), held, part.at[0])
        summing.begin(0)
        for phase in range(summing.steps(True)):
            summing.advance(0, phase, True)
        summing.arrive(0)
        blocks = []

    near_send, near_recv, end_send, end_recv = sems[12:]
    near = {"row": row_pos + 1 - 2 * (row_pos % 2)}

    def send(block):
        start = block * NB // 128 * 128
        rows = slice(block * NB, (block + 1) * NB)
        source, target = upper.at[rows, start:], sibling.at[rows, start:]
        return remote(source, target, near_send.at[block], near_recv.at[block], near)

    def done_block(block, begin, end, rows):
        keep = lax.broadcasted_iota(jnp.int32, rows.shape, 1) >= begin + lax.broadcasted_iota(
            jnp.int32, rows.shape, 0
        )
        upper[begin:end, :] = jnp.where(keep, rows, 0.0)
        send(block).start()

    bound = bound_ref[...]
    samples = window[...].reshape(columns, span)
    place_of = lax.broadcasted_iota(jnp.int32, (columns, span), 1) + core * low
    masked = jnp.where((1 - 2 * core) * (bound - place_of) + core > 0, samples, 0.0)
    rows_of_leaf = (1 - core) * bound + core * (window_rows - bound)
    factor(mm3(masked, masked, NT) / rows_of_leaf.astype(jnp.float32), work, done_block)

    pair_rows = pl.ds(pl.multiple_of(plane.chip * 2 * width, 2 * width), 2 * width)
    give_bases = remote(
        bases_out.at[1 - core], bases_in.at[core], end_send.at[0], end_recv.at[0], plane.partner
    )
    give_coupling = remote(
        coupling_out.at[1 - core], coupling_in.at[core], end_send.at[1], end_recv.at[1], plane.partner
    )
    bases_out[...] = mm3(work[pair_rows, columns:], samples).reshape(bases_out.shape)
    give_bases.start()
    own = upper[pair_rows, :]
    for block in range(columns // NB):
        start = block * NB // 128 * 128
        send(block).wait_recv()
        piece = mm3(own[:, start:], sibling[block * NB : (block + 1) * NB, start:], NT)
        coupling_out[:, :, block * NB : (block + 1) * NB] = piece.reshape(2, width, NB)
    give_coupling.start()
    bases_in[core] = bases_out[core]
    coupling_ref[0, core] = coupling_out[core]
    remote(
        bases_out.at[core], bases_in.at[1 - core], end_send.at[0], end_recv.at[0], plane.partner
    ).wait_recv()
    bases_ref[:, :low] = bases_in[0, :, :low]
    bases_ref[:, span:] = bases_in[1, :, span - low :]
    lane = lax.broadcasted_iota(jnp.int32, (width, span - low), 1) + low
    bases_ref[:, low:span] = jnp.where(lane < bound, bases_in[0, :, low:], bases_in[1, :, : span - low])
    remote(
        coupling_out.at[core], coupling_in.at[1 - core], end_send.at[1], end_recv.at[1], plane.partner
    ).wait_recv()
    coupling_ref[0, 1 - core] = coupling_in[1 - core]

    gather.drain()
    for n in blocks:
        summing.drain(block_of(n), double(n))
    if not blocks:
        summing.drain(0, True)
    for block in range(columns // NB):
        send(block).wait_send()
    give_bases.wait_send()
    give_coupling.wait_send()


def deliver_kernel(bases_ref, coupling_ref, bases_out, coupling_out):
    bases_out[...] = bases_ref[...]
    coupling_out[...] = coupling_ref[...]


def local(contrib, assembled, pattern, omega, row_maps, leaf_bounds):
    tile_rows, tile_cols = contrib.shape[1:]
    window_rows, own_width = omega.shape
    rows = lax.axis_size("row")
    cols = lax.axis_size("col")
    chips = cols * lax.axis_size("child") // 2
    columns = own_width * rows
    width = columns // (2 * chips)
    phases = 1 + (cols // 2).bit_length() - 1
    span = (window_rows // 2 + window_rows // 16 + 127) // 128 * 128
    own = omega.T.reshape(2, own_width // 2, window_rows)
    f32, bf16, dma = jnp.float32, jnp.bfloat16, pltpu.SemaphoreType.DMA
    any_space = pl.BlockSpec(memory_space=pl.ANY)
    stages = rows if own_width >= 8 * SUB else 1
    depth = columns // stages
    chunks = own_width // 2 // CHUNK
    bases, coupling = pl.pallas_call(
        whole_kernel,
        out_shape=(
            jax.ShapeDtypeStruct((width, window_rows), f32),
            jax.ShapeDtypeStruct((1, 2, width, columns), f32),
        ),
        in_specs=[VMEM] + [any_space] * 5,
        out_specs=(VMEM, VMEM),
        scratch_shapes=[
            pltpu.SMEM(pattern.shape, jnp.int32),
            pltpu.VMEM(row_maps.shape, jnp.int32),
            pltpu.VMEM((rows, 2, own_width // 2, window_rows), f32),
            pltpu.VMEM((tile_rows, tile_cols), f32),
            pltpu.VMEM((tile_rows, window_rows), f32),
            pltpu.VMEM((window_rows, tile_cols), bf16),
            pltpu.VMEM((window_rows, tile_rows), bf16),
            pltpu.VMEM((2, tile_rows, tile_cols), bf16),
            pltpu.VMEM((2, tile_rows, window_rows), bf16),
            pltpu.VMEM((stages, depth, window_rows), f32),
            pltpu.VMEM((stages, phases, depth, window_rows // 2), f32),
            pltpu.VMEM((stages, depth, window_rows // 2), f32),
            pltpu.VMEM((stages, phases, depth, window_rows // 2), f32),
            pltpu.VMEM((stages, depth, span), f32),
            pltpu.VMEM((columns, 2 * columns), f32),
            pltpu.VMEM((columns, columns), f32),
            pltpu.VMEM((columns, columns), f32),
            pltpu.VMEM((2, width, span), f32),
            pltpu.VMEM((2, width, span), f32),
            pltpu.VMEM((2, width, columns), f32),
            pltpu.VMEM((2, width, columns), f32),
            dma((4,)),
        ]
        + [dma((rows, chunks))] * 5
        + [dma]
        + [dma((stages,))] * 2
        + [dma((stages, max(phases, 3), 2))] * 2
        + [dma((stages,))] * 2
        + [dma((columns // NB,))] * 2
        + [dma((2,))] * 2,
        compiler_params=pltpu.CompilerParams(
            collective_id=0, has_side_effects=True, vmem_limit_bytes=(64 << 20) - ROOM
        ),
        name="front_samples",
    )(leaf_bounds.reshape(1, 1), pattern, own, contrib, assembled, row_maps)
    bases, coupling = pl.pallas_call(
        deliver_kernel,
        out_shape=(
            jax.ShapeDtypeStruct(bases.shape, f32),
            jax.ShapeDtypeStruct(coupling.shape, f32),
        ),
        in_specs=[VMEM, VMEM],
        out_specs=(VMEM, VMEM),
        compiler_params=pltpu.CompilerParams(vmem_limit_bytes=SMALL),
        name="deliver",
    )(bases, coupling)
    return (bases.T, coupling)


def solution(mesh):
    in_specs = (
        P("child", "row", "col"),
        P("child", "row", "col"),
        P("row", "col"),
        P("col", "row"),
        P("child", None),
        P("row"),
    )
    out_specs = (P("row", ("child", "col")), P("row", None, ("child", "col"), None))
    return jax.shard_map(local, mesh=mesh, in_specs=in_specs, out_specs=out_specs, check_vma=False)
```

```python
import jax
import jax.numpy as jnp
from jax import lax
from jax.experimental import pallas as pl
from jax.experimental.pallas import tpu as pltpu
from jax.sharding import PartitionSpec as P

BT = 256
NB = 128
PIECE = 64
SUB = 8
CHUNK = 8
TWINS = 1
ROOM = 8 << 20
SMALL = 62 << 20
DOUBLED = 1
MESH = pl.DeviceIdType.MESH
VMEM = pl.BlockSpec(memory_space=pltpu.VMEM)
SMEM = pl.BlockSpec(memory_space=pltpu.SMEM)

NN = (((1,), (0,)), ((), ()))
NT = (((1,), (1,)), ((), ()))
TN = (((0,), (0,)), ((), ()))


def split(a):
    high = a.astype(jnp.bfloat16)
    low = (a - high.astype(jnp.float32)).astype(jnp.bfloat16)
    return high, low


def dot16(a, b, dims=NN):
    return lax.dot_general(a, b, dims, preferred_element_type=jnp.float32)


def mm3(a, b, dims=NN):
    (ah, al), (bh, bl) = split(a), split(b)
    return dot16(ah, bh, dims) + (dot16(ah, bl, dims) + dot16(al, bh, dims))


class Plane:
    def __init__(self):
        self.cols = lax.axis_size("col")
        self.chips = self.cols * lax.axis_size("child") // 2
        self.child = lax.axis_index("child")
        self.col = lax.axis_index("col")
        self.core = self.col % 2
        self.chip = (self.child * self.cols + self.col) // 2
        self.partner = {"col": self.col + 1 - 2 * self.core}
        self.across = [{"child": 1 - self.child}]
        step = 2
        while step < self.cols:
            self.across.append({"col": self.col + step - 2 * step * (self.col // step % 2)})
            step *= 2
        self.high = self.col // 2 % 2


def remote(source, target, send_sem, recv_sem, device):
    return pltpu.make_async_remote_copy(
        src_ref=source, dst_ref=target, send_sem=send_sem, recv_sem=recv_sem, device_id=device, device_id_type=MESH
    )


def greet(plane):
    count = lax.axis_size("row")
    me = lax.axis_index("row")
    barrier = pltpu.get_barrier_semaphore()

    @pl.when(me > 0)
    def _():
        pl.semaphore_signal(barrier, inc=1, device_id={"row": me - 1}, device_id_type=MESH)

    @pl.when(me < count - 1)
    def _():
        pl.semaphore_signal(barrier, inc=1, device_id={"row": me + 1}, device_id_type=MESH)

    near = [plane.partner] + plane.across
    for device in near:
        pl.semaphore_signal(barrier, inc=1, device_id=device, device_id_type=MESH)
    pl.semaphore_wait(barrier, len(near) + jnp.minimum(me, 1) + jnp.minimum(count - 1 - me, 1))


class Gather:
    def __init__(self, own_ref, out_ref, sems):
        self.own, self.out = own_ref, out_ref
        self.send_right, self.send_left, self.recv, self.swap_send, self.swap_recv = sems[:5]
        self.twin_send, self.twin_recv, self.local_sem = sems[5:]
        self.count = lax.axis_size("row")
        self.me = lax.axis_index("row")
        self.half = lax.axis_index("child")
        self.chunks = own_ref.shape[1] // CHUNK
        self.first_twin = self.chunks - min(TWINS, self.chunks - 1)
        self.has_left = self.me > 0
        self.has_right = self.me < self.count - 1

    def rows(self, chunk):
        return slice(chunk * CHUNK, (chunk + 1) * CHUNK)

    def hop(self, block, target, step, send, chunk):
        place = self.out.at[block, self.half, self.rows(chunk)]
        source = self.own.at[self.half, self.rows(chunk)] if step == 0 else place
        return remote(source, place, send.at[block, chunk], self.recv.at[block, chunk], {"row": target})

    def swap(self, block, chunk, half):
        place = self.out.at[block, half, self.rows(chunk)]
        sems = (self.swap_send.at[block, chunk], self.swap_recv.at[block, chunk])
        return remote(place, place, *sems, {"child": 1 - self.half})

    def twin(self, block, target, step, chunk):
        place = self.out.at[block, 1 - self.half, self.rows(chunk)]
        source = self.own.at[1 - self.half, self.rows(chunk)] if step == 0 else place
        sems = (self.twin_send.at[block, chunk], self.twin_recv.at[block, chunk])
        return remote(source, place, *sems, {"row": target})

    def pass_on(self, step, chunk):
        low, high = self.me - step, self.me + step
        ways = (
            (low, low >= 0, low == 0, self.has_right, 1, self.send_right),
            (high, high < self.count, high == self.count - 1, self.has_left, -1, self.send_left),
        )
        for block, there, outer, onward, way, sems in ways:
            if step > 0:

                @pl.when(there)
                def _():
                    self.hop(block, self.me - way, step, sems, chunk).wait_recv()

            @pl.when(jnp.logical_and(there, onward))
            def _():
                self.hop(block, self.me + way, step, sems, chunk).start()

            if chunk >= self.first_twin:
                if step > 0:

                    @pl.when(outer)
                    def _():
                        self.twin(block, self.me - way, step, chunk).wait_recv()

                @pl.when(jnp.logical_and(outer, onward))
                def _():
                    self.twin(block, self.me + way, step, chunk).start()

            if step > 0:
                inner = jnp.logical_and(there, jnp.logical_not(outer))

                @pl.when(inner if chunk >= self.first_twin else there)
                def _():
                    self.swap(block, chunk, self.half).start()

    def run(self, work):
        keep = pltpu.make_async_copy(self.own, self.out.at[self.me], self.local_sem)
        keep.start()
        for step in range(self.count):
            for chunk in range(self.chunks):
                self.pass_on(step, chunk)
                if step == 0 and chunk == self.chunks - 1:
                    keep.wait()
                for act in work.get((step, chunk), ()):
                    act()

    def nth(self, n):
        left, right = self.me, self.count - 1 - self.me
        both = jnp.minimum(left, right)
        near = (n + 1) // 2
        beside = self.me - near if n % 2 == 1 else self.me + near
        beyond = jnp.where(left < right, self.me + n - both, self.me - n + both)
        return jnp.where(n <= 2 * both, beside, beyond)

    def swapped(self, block, chunk, act):
        if chunk < self.first_twin:
            act()
        else:
            pl.when(jnp.logical_and(block > 0, block < self.count - 1))(act)

    def arrive(self, block):
        for chunk in range(self.chunks):
            self.swapped(block, chunk, lambda: self.swap(block, chunk, 1 - self.half).wait_recv())

    def drain(self):
        for step in range(self.count):
            low, high = self.me - step, self.me + step
            ways = (
                (low, low >= 0, low == 0, self.has_right, 1, self.send_right),
                (high, high < self.count, high == self.count - 1, self.has_left, -1, self.send_left),
            )
            for chunk in range(self.chunks):
                for block, there, outer, onward, way, sems in ways:

                    @pl.when(jnp.logical_and(there, onward))
                    def _():
                        self.hop(block, self.me + way, step, sems, chunk).wait_send()

                    if chunk >= self.first_twin:

                        @pl.when(jnp.logical_and(outer, onward))
                        def _():
                            self.twin(block, self.me + way, step, chunk).wait_send()

        for step in range(1, self.count):
            block = lax.rem(self.me + step, self.count)
            for chunk in range(self.chunks):
                self.swapped(block, chunk, lambda: self.swap(block, chunk, self.half).wait_send())


def prepare_sketch(pattern_ref, contrib, assembled, maps_ref, held):
    pick, place, front, entries = held
    half = lax.axis_index("child")
    tile_rows, tile_cols = contrib.shape
    window_rows = assembled.shape[1]
    row_pos, col_pos = lax.axis_index("row"), lax.axis_index("col")
    columns = maps_ref[:, pl.ds(pl.multiple_of(col_pos * tile_cols, tile_cols), tile_cols)] - col_pos * window_rows
    targets = maps_ref[:, pl.ds(pl.multiple_of(row_pos * tile_rows, tile_rows), tile_rows)] - row_pos * window_rows
    index = lax.broadcasted_iota(jnp.int32, (window_rows, tile_cols), 0)
    pick[...] = jnp.where(index == columns, 1.0, 0.0).astype(jnp.bfloat16)
    index = lax.broadcasted_iota(jnp.int32, (window_rows, tile_rows), 0)
    place[...] = jnp.where(index == targets, 1.0, 0.0).astype(jnp.bfloat16)
    front[0], front[1] = split(contrib[...])
    for row in range(tile_rows // BT):
        for col in range(window_rows // BT):
            where = (slice(row * BT, (row + 1) * BT), slice(col * BT, (col + 1) * BT))
            present = pattern_ref[half * (tile_rows // BT) + row, col].astype(jnp.float32)
            entries[(0,) + where], entries[(1,) + where] = split(assembled[where] * present)


def stacked(a, b, dims=NN):
    rows = a.shape[0] // 2
    both = dot16(a, b[0], dims)
    return both[:rows] + (dot16(a[:rows], b[1], dims) + both[rows:])


def sketch(omega, held, part_ref):
    pick, place, front, entries = held
    half = lax.axis_index("child")
    rows, tile_rows = omega.shape[0], place.shape[1]
    both = jnp.concatenate(split(omega), axis=0)
    picked = dot16(both, pick[...]).astype(jnp.bfloat16)
    product = stacked(picked, front, NT)
    sparse = stacked(both, entries, NT)
    spread = dot16(jnp.concatenate(split(product), axis=0), place[...], NT)
    part_ref[...] = spread[:rows] + spread[rows:]
    where = pl.ds(pl.multiple_of(half * tile_rows, tile_rows), tile_rows)
    part_ref[:, where] = part_ref[:, where] + sparse


class Total:
    def __init__(self, plane, part, sums, pair_buf, landed, window, sems):
        self.plane, self.part, self.sums, self.pair_buf = plane, part, sums, pair_buf
        self.landed, self.window = landed, window
        self.pair_send, self.pair_recv, self.send, self.recv, self.hand_send, self.hand_recv = sems
        self.phases = len(plane.across)
        self.depth, self.half = pair_buf.shape[1:]
        self.shared = window.shape[2] - self.half
        self.place = self.lanes(plane.core * self.shared, self.half)

    def lanes(self, offset, size):
        return pl.ds(pl.multiple_of(offset, 128), size)

    def side(self, which):
        return pl.ds(pl.multiple_of(which * (self.depth // 2), SUB), self.depth // 2)

    def pair(self, r):
        source = self.part.at[r, :, self.lanes((1 - self.plane.core) * self.half, self.half)]
        return remote(source, self.pair_buf.at[r], self.pair_send.at[r], self.pair_recv.at[r], self.plane.partner)

    def hand(self, r):
        core, half, shared = self.plane.core, self.half, self.shared
        source = self.window.at[r, :, self.lanes((1 - core) * (half - shared) + core * shared, shared)]
        target = self.window.at[r, :, self.lanes(core * half, shared)]
        return remote(source, target, self.hand_send.at[r], self.hand_recv.at[r], self.plane.partner)

    def cross(self, r, phase, side):
        device = self.plane.across[(phase + side) % self.phases]
        rows = self.side(side)
        sems = (self.send.at[r, phase, side], self.recv.at[r, phase, side])
        return remote(self.sums.at[r, phase, rows], self.landed.at[r, phase, rows], *sems, device)

    def scatter(self, r, phase, arriving=False):
        keep, away = self.plane.high, 1 - self.plane.high
        sems = (self.send.at[r, phase, 0], self.recv.at[r, phase, 0])
        if phase == 0:
            rows = self.side(keep if arriving else away)
            return remote(self.sums.at[r, 0, rows], self.landed.at[r, 0, rows], *sems, self.plane.across[1])
        if phase == 1:
            rows = self.side(keep)
            return remote(self.sums.at[r, 1, rows], self.landed.at[r, 1, rows], *sems, self.plane.across[0])
        place = self.window.at[r, self.side(away if arriving else keep), self.place]
        return remote(place, place, *sems, self.plane.across[1])

    def begin(self, r):
        self.pair(r).start()

    def steps(self, double):
        return self.phases + 1 if double else 4

    def advance(self, r, phase, double):
        if phase == 0:
            self.pair(r).wait_recv()
            own = self.lanes(self.plane.core * self.half, self.half)
            self.sums[r, 0] = self.part[r, :, own] + self.pair_buf[r]
            if double:
                for side in range(2):
                    self.cross(r, 0, side).start()
            else:
                self.scatter(r, 0).start()
            return
        if double:
            for side in range(2):
                rows = self.side(side)
                self.cross(r, phase - 1, side).wait_recv()
                total = self.sums[r, phase - 1, rows] + self.landed[r, phase - 1, rows]
                if phase < self.phases:
                    self.sums[r, phase, rows] = total
                    self.cross(r, phase, side).start()
                else:
                    self.window[r, rows, self.place] = total
            if phase == self.phases:
                self.hand(r).start()
            return
        self.scatter(r, phase - 1, True).wait_recv()
        if phase == 3:
            self.hand(r).start()
            return
        rows = self.side(self.plane.high)
        total = self.sums[r, phase - 1, rows] + self.landed[r, phase - 1, rows]
        if phase == 1:
            self.sums[r, 1, rows] = total
        else:
            self.window[r, rows, self.place] = total
        self.scatter(r, phase).start()

    def arrive(self, r):
        core, half, shared = self.plane.core, self.half, self.shared
        target = self.window.at[r, :, self.lanes((1 - core) * half, shared)]
        remote(target, target, self.hand_send.at[r], self.hand_recv.at[r], self.plane.partner).wait_recv()

    def drain(self, r, double):
        self.pair(r).wait_send()
        self.hand(r).wait_send()
        if double:
            for phase in range(self.phases):
                for side in range(2):
                    self.cross(r, phase, side).wait_send()
        else:
            for phase in range(3):
                self.scatter(r, phase).wait_send()


def eliminate(rows, finish):
    groups = len(rows)
    wide = rows[0].shape
    index = lax.broadcasted_iota(jnp.int32, wide, 0)
    rows = list(rows)
    for panel in range(groups):
        first = panel * SUB
        cols = {
            q: [jnp.broadcast_to(rows[q][:, first + k : first + k + 1], wide) for k in range(SUB)]
            for q in range(panel, groups)
        }
        own = cols[panel]
        square = jnp.broadcast_to(own[0][0:1], wide)
        for k in range(SUB):
            scale = lax.rsqrt(square)
            if k + 1 < SUB:
                beside = jnp.broadcast_to(own[k][k + 1 : k + 2], wide) * scale
                square = jnp.broadcast_to(own[k + 1][k + 1 : k + 2], wide) - beside * beside
            pivot = jnp.broadcast_to(rows[panel][k : k + 1], wide) * scale
            weight = {q: cols[q][k] * scale for q in range(panel, groups)}
            across = weight[panel]
            below = jnp.where(index > k, across, 0.0)
            rows[panel] = jnp.where(index == k, pivot, rows[panel] - below * pivot)
            for j in range(k + 1, SUB):
                factor = jnp.broadcast_to(across[j : j + 1], wide)
                for q in range(panel, groups):
                    cols[q][j] = cols[q][j] - (below if q == panel else weight[q]) * factor
            for q in range(panel + 1, groups):
                rows[q] = rows[q] - weight[q] * pivot
        finish(panel, rows[panel])
    return rows


def factor(gram, work, upper, send):
    columns = gram.shape[0]
    eye = jnp.where(
        lax.broadcasted_iota(jnp.int32, (columns, columns), 0)
        == lax.broadcasted_iota(jnp.int32, (columns, columns), 1),
        1.0,
        0.0,
    )
    work[:, :columns] = gram
    work[:, columns:] = eye
    diagonal = gram[:NB, :NB]
    for block in range(columns // NB):
        begin, end = block * NB, (block + 1) * NB
        if begin > 0:
            upper[begin:end, :begin] = jnp.zeros((NB, begin), jnp.float32)

        def finish(panel, values):
            start = panel * SUB
            lane = lax.broadcasted_iota(jnp.int32, (SUB, NB), 1)
            row = lax.broadcasted_iota(jnp.int32, (SUB, NB), 0) + start
            upper[begin + start : begin + start + SUB, begin:end] = jnp.where(lane >= row, values[:, :NB], 0.0)
            if end == columns and (start + SUB) % PIECE == 0:
                send((begin + start) // PIECE).start()

        both = jnp.concatenate([diagonal, eye[:NB, :NB]], axis=1)
        done = eliminate([both[q * SUB : (q + 1) * SUB] for q in range(NB // SUB)], finish)
        inverse = jnp.concatenate(done, axis=0)[:, NB:]
        if end < columns:
            right = mm3(inverse, work[begin:end, end:columns])
            rest = work[end:, end:columns] - mm3(right, right, TN)
            diagonal = rest[:NB, :NB]
            work[end:, end:columns] = rest
            upper[begin:end, end:] = right
            for piece in range(begin // PIECE, end // PIECE):
                send(piece).start()
        left = mm3(inverse, work[begin:end, columns:])
        work[begin:end, columns:] = left
        if end < columns:
            work[end:, columns:] = work[end:, columns:] - mm3(right, left, TN)


def whole_kernel(
    bound_ref, pattern_hbm, omega_ref, contrib_ref, assembled_ref, maps_hbm, bases_ref, coupling_ref,
    pattern_ref, maps_ref, gathered, contrib_buf, assembled_buf, pick, place, front, entries,
    part, sums, pair_buf, landed, window, work, upper, sibling, bases_out, bases_in, coupling_out, coupling_in,
    input_sems, *sems,
):
    plane = Plane()
    core = plane.core
    window_rows = assembled_buf.shape[1]
    columns, width = upper.shape[1], bases_ref.shape[0]
    stages, span = window.shape[0], window.shape[2]
    low = window_rows - span
    held = (pick, place, front, entries)
    load_front = pltpu.make_async_copy(contrib_ref.at[0], contrib_buf, input_sems.at[0])
    load_entries = pltpu.make_async_copy(assembled_ref.at[0], assembled_buf, input_sems.at[1])
    load_small = [
        pltpu.make_async_copy(source, target, input_sems.at[2 + i])
        for i, (source, target) in enumerate(
            ((maps_hbm, maps_ref), (pattern_hbm, pattern_ref))
        )
    ]
    for copy in load_small + [load_front, load_entries]:
        copy.start()
    greet(plane)

    row_count, row_pos = lax.axis_size("row"), lax.axis_index("row")
    gather = Gather(omega_ref, gathered, sems[:8])
    summing = Total(plane, part, sums, pair_buf, landed, window, sems[8:14])

    def prepare():
        for copy in load_small + [load_front, load_entries]:
            copy.wait()
        prepare_sketch(pattern_ref, contrib_buf, assembled_buf, maps_ref, held)

    def block_of(n):
        return row_pos if n == 0 else gather.nth(n)

    def double(n):
        return n >= stages - DOUBLED

    def stage(n):
        block = block_of(n)
        if n > 0:
            gather.arrive(block)
        sketch(gathered[block].reshape(columns // stages, window_rows), held, part.at[block])
        summing.begin(block)

    if stages == row_count:
        begun, left = [], {}

        def begin(n):
            stage(n)
            begun.append(n)
            left[n] = list(range(summing.steps(double(n))))

        def go(n):
            if n in left and left[n]:
                summing.advance(block_of(n), left[n].pop(0), double(n))

        def go_all():
            for n in list(begun):
                go(n)

        end, mid = gather.chunks - 1, gather.chunks // 2
        queue = {(0, end): [prepare, lambda: begin(0)]}
        queue.setdefault((1, mid), []).append(lambda: go(0))
        queue.setdefault((2, end), []).append(lambda: go(0))
        if row_count > 3:
            queue.setdefault((3, 0), []).append(lambda: begin(1))
        gather.run(queue)
        go(1)
        for n in range(len(begun), stages):
            begin(n)
            go_all()
        while any(left.values()):
            go_all()
        blocks = range(stages)
        for n in blocks:
            summing.arrive(block_of(n))
    else:
        gather.run({(0, 0): [prepare]})
        for step in range(1, row_count):
            gather.arrive(lax.rem(row_pos + step, row_count))
        sketch(gathered[...].reshape(columns, window_rows), held, part.at[0])
        summing.begin(0)
        for phase in range(summing.steps(True)):
            summing.advance(0, phase, True)
        summing.arrive(0)
        blocks = []

    near_send, near_recv, end_send, end_recv = sems[14:]
    near = {"row": row_pos + 1 - 2 * (row_pos % 2)}

    def send(piece):
        start = piece * PIECE // 128 * 128
        rows = slice(piece * PIECE, (piece + 1) * PIECE)
        source, target = upper.at[rows, start:], sibling.at[rows, start:]
        return remote(source, target, near_send.at[piece], near_recv.at[piece], near)

    bound = bound_ref[...]
    samples = window[...].reshape(columns, span)
    place_of = lax.broadcasted_iota(jnp.int32, (columns, span), 1) + core * low
    masked = jnp.where((1 - 2 * core) * (bound - place_of) + core > 0, samples, 0.0)
    rows_of_leaf = (1 - core) * bound + core * (window_rows - bound)
    factor(mm3(masked, masked, NT) / rows_of_leaf.astype(jnp.float32), work, upper, send)

    pair_rows = pl.ds(pl.multiple_of(plane.chip * 2 * width, 2 * width), 2 * width)
    give_bases = remote(
        bases_out.at[1 - core], bases_in.at[core], end_send.at[0], end_recv.at[0], plane.partner
    )
    give_coupling = remote(
        coupling_out.at[1 - core], coupling_in.at[core], end_send.at[1], end_recv.at[1], plane.partner
    )
    bases_out[...] = mm3(work[pair_rows, columns:], samples).reshape(bases_out.shape)
    give_bases.start()
    own = upper[pair_rows, :]
    for piece in range(columns // PIECE):
        start = piece * PIECE // 128 * 128
        rows = slice(piece * PIECE, (piece + 1) * PIECE)
        send(piece).wait_recv()
        product = mm3(own[:, start:], sibling[rows, start:], NT)
        coupling_out[:, :, rows] = product.reshape(2, width, PIECE)
    give_coupling.start()
    bases_in[core] = bases_out[core]
    coupling_ref[0, core] = coupling_out[core]
    remote(
        bases_out.at[core], bases_in.at[1 - core], end_send.at[0], end_recv.at[0], plane.partner
    ).wait_recv()
    bases_ref[:, :low] = bases_in[0, :, :low]
    bases_ref[:, span:] = bases_in[1, :, span - low :]
    lane = lax.broadcasted_iota(jnp.int32, (width, span - low), 1) + low
    bases_ref[:, low:span] = jnp.where(lane < bound, bases_in[0, :, low:], bases_in[1, :, : span - low])
    remote(
        coupling_out.at[core], coupling_in.at[1 - core], end_send.at[1], end_recv.at[1], plane.partner
    ).wait_recv()
    coupling_ref[0, 1 - core] = coupling_in[1 - core]

    gather.drain()
    for n in blocks:
        summing.drain(block_of(n), double(n))
    if not blocks:
        summing.drain(0, True)
    for piece in range(columns // PIECE):
        send(piece).wait_send()
    give_bases.wait_send()
    give_coupling.wait_send()


def deliver_kernel(bases_ref, coupling_ref, bases_out, coupling_out):
    bases_out[...] = bases_ref[...]
    coupling_out[...] = coupling_ref[...]


def local(contrib, assembled, pattern, omega, row_maps, leaf_bounds):
    tile_rows, tile_cols = contrib.shape[1:]
    window_rows, own_width = omega.shape
    rows = lax.axis_size("row")
    cols = lax.axis_size("col")
    chips = cols * lax.axis_size("child") // 2
    columns = own_width * rows
    width = columns // (2 * chips)
    phases = 1 + (cols // 2).bit_length() - 1
    span = (window_rows // 2 + window_rows // 16 + 127) // 128 * 128
    own = omega.T.reshape(2, own_width // 2, window_rows)
    f32, bf16, dma = jnp.float32, jnp.bfloat16, pltpu.SemaphoreType.DMA
    any_space = pl.BlockSpec(memory_space=pl.ANY)
    stages = rows if own_width >= 8 * SUB else 1
    depth = columns // stages
    chunks = own_width // 2 // CHUNK
    bases, coupling = pl.pallas_call(
        whole_kernel,
        out_shape=(
            jax.ShapeDtypeStruct((width, window_rows), f32),
            jax.ShapeDtypeStruct((1, 2, width, columns), f32),
        ),
        in_specs=[VMEM] + [any_space] * 5,
        out_specs=(VMEM, VMEM),
        scratch_shapes=[
            pltpu.SMEM(pattern.shape, jnp.int32),
            pltpu.VMEM(row_maps.shape, jnp.int32),
            pltpu.VMEM((rows, 2, own_width // 2, window_rows), f32),
            pltpu.VMEM((tile_rows, tile_cols), f32),
            pltpu.VMEM((tile_rows, window_rows), f32),
            pltpu.VMEM((window_rows, tile_cols), bf16),
            pltpu.VMEM((window_rows, tile_rows), bf16),
            pltpu.VMEM((2, tile_rows, tile_cols), bf16),
            pltpu.VMEM((2, tile_rows, window_rows), bf16),
            pltpu.VMEM((stages, depth, window_rows), f32),
            pltpu.VMEM((stages, phases, depth, window_rows // 2), f32),
            pltpu.VMEM((stages, depth, window_rows // 2), f32),
            pltpu.VMEM((stages, phases, depth, window_rows // 2), f32),
            pltpu.VMEM((stages, depth, span), f32),
            pltpu.VMEM((columns, 2 * columns), f32),
            pltpu.VMEM((columns, columns), f32),
            pltpu.VMEM((columns, columns), f32),
            pltpu.VMEM((2, width, span), f32),
            pltpu.VMEM((2, width, span), f32),
            pltpu.VMEM((2, width, columns), f32),
            pltpu.VMEM((2, width, columns), f32),
            dma((4,)),
        ]
        + [dma((rows, chunks))] * 7
        + [dma]
        + [dma((stages,))] * 2
        + [dma((stages, max(phases, 3), 2))] * 2
        + [dma((stages,))] * 2
        + [dma((columns // PIECE,))] * 2
        + [dma((2,))] * 2,
        compiler_params=pltpu.CompilerParams(
            collective_id=0, has_side_effects=True, vmem_limit_bytes=(64 << 20) - ROOM
        ),
        name="front_samples",
    )(leaf_bounds.reshape(1, 1), pattern, own, contrib, assembled, row_maps)
    bases, coupling = pl.pallas_call(
        deliver_kernel,
        out_shape=(
            jax.ShapeDtypeStruct(bases.shape, f32),
            jax.ShapeDtypeStruct(coupling.shape, f32),
        ),
        in_specs=[VMEM, VMEM],
        out_specs=(VMEM, VMEM),
        compiler_params=pltpu.CompilerParams(vmem_limit_bytes=SMALL),
        name="deliver",
    )(bases, coupling)
    return (bases.T, coupling)


def solution(mesh):
    in_specs = (
        P("child", "row", "col"),
        P("child", "row", "col"),
        P("row", "col"),
        P("col", "row"),
        P("child", None),
        P("row"),
    )
    out_specs = (P("row", ("child", "col")), P("row", None, ("child", "col"), None))
    return jax.shard_map(local, mesh=mesh, in_specs=in_specs, out_specs=out_specs, check_vma=False)
```

```python
import jax
import jax.numpy as jnp
from jax import lax
from jax.experimental import pallas as pl
from jax.experimental.pallas import tpu as pltpu
from jax.sharding import PartitionSpec as P

BT = 256
NB = 128
PIECE = 64
SUB = 8
CHUNK = 8
TWINS = 1
EARLY = ((1, 2, 0), (2, 3, 0), (3, 0, 11))
LATE = (1, 12, 0, 1, 2, 13, 0, 1, 2, 3)
ROOM = 8 << 20
SMALL = 62 << 20
DOUBLED = 1
MESH = pl.DeviceIdType.MESH
VMEM = pl.BlockSpec(memory_space=pltpu.VMEM)
SMEM = pl.BlockSpec(memory_space=pltpu.SMEM)

NN = (((1,), (0,)), ((), ()))
NT = (((1,), (1,)), ((), ()))
TN = (((0,), (0,)), ((), ()))


def split(a):
    high = a.astype(jnp.bfloat16)
    low = (a - high.astype(jnp.float32)).astype(jnp.bfloat16)
    return high, low


def dot16(a, b, dims=NN):
    return lax.dot_general(a, b, dims, preferred_element_type=jnp.float32)


def mm3(a, b, dims=NN):
    (ah, al), (bh, bl) = split(a), split(b)
    return dot16(ah, bh, dims) + (dot16(ah, bl, dims) + dot16(al, bh, dims))


class Plane:
    def __init__(self):
        self.cols = lax.axis_size("col")
        self.chips = self.cols * lax.axis_size("child") // 2
        self.child = lax.axis_index("child")
        self.col = lax.axis_index("col")
        self.core = self.col % 2
        self.chip = (self.child * self.cols + self.col) // 2
        self.partner = {"col": self.col + 1 - 2 * self.core}
        self.across = [{"child": 1 - self.child}]
        step = 2
        while step < self.cols:
            self.across.append({"col": self.col + step - 2 * step * (self.col // step % 2)})
            step *= 2
        self.high = self.col // 2 % 2


def remote(source, target, send_sem, recv_sem, device):
    return pltpu.make_async_remote_copy(
        src_ref=source, dst_ref=target, send_sem=send_sem, recv_sem=recv_sem, device_id=device, device_id_type=MESH
    )


def greet(plane):
    count = lax.axis_size("row")
    me = lax.axis_index("row")
    barrier = pltpu.get_barrier_semaphore()

    @pl.when(me > 0)
    def _():
        pl.semaphore_signal(barrier, inc=1, device_id={"row": me - 1}, device_id_type=MESH)

    @pl.when(me < count - 1)
    def _():
        pl.semaphore_signal(barrier, inc=1, device_id={"row": me + 1}, device_id_type=MESH)

    near = [plane.partner] + plane.across
    for device in near:
        pl.semaphore_signal(barrier, inc=1, device_id=device, device_id_type=MESH)
    pl.semaphore_wait(barrier, len(near) + jnp.minimum(me, 1) + jnp.minimum(count - 1 - me, 1))


class Gather:
    def __init__(self, own_ref, out_ref, sems):
        self.own, self.out = own_ref, out_ref
        self.send_right, self.send_left, self.recv, self.swap_send, self.swap_recv = sems[:5]
        self.twin_send, self.twin_recv, self.local_sem = sems[5:]
        self.count = lax.axis_size("row")
        self.me = lax.axis_index("row")
        self.half = lax.axis_index("child")
        self.chunks = own_ref.shape[1] // CHUNK
        self.first_twin = self.chunks - min(TWINS, self.chunks - 1)
        self.has_left = self.me > 0
        self.has_right = self.me < self.count - 1

    def rows(self, chunk):
        return slice(chunk * CHUNK, (chunk + 1) * CHUNK)

    def hop(self, block, target, step, send, chunk):
        place = self.out.at[block, self.half, self.rows(chunk)]
        source = self.own.at[self.half, self.rows(chunk)] if step == 0 else place
        return remote(source, place, send.at[block, chunk], self.recv.at[block, chunk], {"row": target})

    def swap(self, block, chunk, half):
        place = self.out.at[block, half, self.rows(chunk)]
        sems = (self.swap_send.at[block, chunk], self.swap_recv.at[block, chunk])
        return remote(place, place, *sems, {"child": 1 - self.half})

    def twin(self, block, target, step, chunk):
        place = self.out.at[block, 1 - self.half, self.rows(chunk)]
        source = self.own.at[1 - self.half, self.rows(chunk)] if step == 0 else place
        sems = (self.twin_send.at[block, chunk], self.twin_recv.at[block, chunk])
        return remote(source, place, *sems, {"row": target})

    def pass_on(self, step, chunk):
        low, high = self.me - step, self.me + step
        ways = (
            (low, low >= 0, low == 0, self.has_right, 1, self.send_right),
            (high, high < self.count, high == self.count - 1, self.has_left, -1, self.send_left),
        )
        for block, there, outer, onward, way, sems in ways:
            if step > 0:

                @pl.when(there)
                def _():
                    self.hop(block, self.me - way, step, sems, chunk).wait_recv()

            @pl.when(jnp.logical_and(there, onward))
            def _():
                self.hop(block, self.me + way, step, sems, chunk).start()

            if chunk >= self.first_twin:
                if step > 0:

                    @pl.when(outer)
                    def _():
                        self.twin(block, self.me - way, step, chunk).wait_recv()

                @pl.when(jnp.logical_and(outer, onward))
                def _():
                    self.twin(block, self.me + way, step, chunk).start()

            if step > 0:
                inner = jnp.logical_and(there, jnp.logical_not(outer))

                @pl.when(inner if chunk >= self.first_twin else there)
                def _():
                    self.swap(block, chunk, self.half).start()

    def run(self, work):
        keep = pltpu.make_async_copy(self.own, self.out.at[self.me], self.local_sem)
        keep.start()
        for step in range(self.count):
            for chunk in range(self.chunks):
                self.pass_on(step, chunk)
                if step == 0 and chunk == self.chunks - 1:
                    keep.wait()
                for act in work.get((step, chunk), ()):
                    act()

    def nth(self, n):
        left, right = self.me, self.count - 1 - self.me
        both = jnp.minimum(left, right)
        near = (n + 1) // 2
        beside = self.me - near if n % 2 == 1 else self.me + near
        beyond = jnp.where(left < right, self.me + n - both, self.me - n + both)
        return jnp.where(n <= 2 * both, beside, beyond)

    def swapped(self, block, chunk, act):
        if chunk < self.first_twin:
            act()
        else:
            pl.when(jnp.logical_and(block > 0, block < self.count - 1))(act)

    def arrive(self, block):
        for chunk in range(self.chunks):
            self.swapped(block, chunk, lambda: self.swap(block, chunk, 1 - self.half).wait_recv())

    def drain(self):
        for step in range(self.count):
            low, high = self.me - step, self.me + step
            ways = (
                (low, low >= 0, low == 0, self.has_right, 1, self.send_right),
                (high, high < self.count, high == self.count - 1, self.has_left, -1, self.send_left),
            )
            for chunk in range(self.chunks):
                for block, there, outer, onward, way, sems in ways:

                    @pl.when(jnp.logical_and(there, onward))
                    def _():
                        self.hop(block, self.me + way, step, sems, chunk).wait_send()

                    if chunk >= self.first_twin:

                        @pl.when(jnp.logical_and(outer, onward))
                        def _():
                            self.twin(block, self.me + way, step, chunk).wait_send()

        for step in range(1, self.count):
            block = lax.rem(self.me + step, self.count)
            for chunk in range(self.chunks):
                self.swapped(block, chunk, lambda: self.swap(block, chunk, self.half).wait_send())


def prepare_sketch(pattern_ref, contrib, assembled, maps_ref, held):
    pick, place, front, entries = held
    half = lax.axis_index("child")
    tile_rows, tile_cols = contrib.shape
    window_rows = assembled.shape[1]
    row_pos, col_pos = lax.axis_index("row"), lax.axis_index("col")
    columns = maps_ref[:, pl.ds(pl.multiple_of(col_pos * tile_cols, tile_cols), tile_cols)] - col_pos * window_rows
    targets = maps_ref[:, pl.ds(pl.multiple_of(row_pos * tile_rows, tile_rows), tile_rows)] - row_pos * window_rows
    index = lax.broadcasted_iota(jnp.int32, (window_rows, tile_cols), 0)
    pick[...] = jnp.where(index == columns, 1.0, 0.0).astype(jnp.bfloat16)
    index = lax.broadcasted_iota(jnp.int32, (window_rows, tile_rows), 0)
    place[...] = jnp.where(index == targets, 1.0, 0.0).astype(jnp.bfloat16)
    front[0], front[1] = split(contrib[...])
    for row in range(tile_rows // BT):
        for col in range(window_rows // BT):
            where = (slice(row * BT, (row + 1) * BT), slice(col * BT, (col + 1) * BT))
            present = pattern_ref[half * (tile_rows // BT) + row, col].astype(jnp.float32)
            entries[(0,) + where], entries[(1,) + where] = split(assembled[where] * present)


def stacked(a, b, dims=NN):
    rows = a.shape[0] // 2
    both = dot16(a, b[0], dims)
    return both[:rows] + (dot16(a[:rows], b[1], dims) + both[rows:])


def sketch(omega, held, part_ref):
    pick, place, front, entries = held
    half = lax.axis_index("child")
    rows, tile_rows = omega.shape[0], place.shape[1]
    both = jnp.concatenate(split(omega), axis=0)
    picked = dot16(both, pick[...]).astype(jnp.bfloat16)
    product = stacked(picked, front, NT)
    sparse = stacked(both, entries, NT)
    spread = dot16(jnp.concatenate(split(product), axis=0), place[...], NT)
    part_ref[...] = spread[:rows] + spread[rows:]
    where = pl.ds(pl.multiple_of(half * tile_rows, tile_rows), tile_rows)
    part_ref[:, where] = part_ref[:, where] + sparse


class Total:
    def __init__(self, plane, part, sums, pair_buf, landed, window, sems):
        self.plane, self.part, self.sums, self.pair_buf = plane, part, sums, pair_buf
        self.landed, self.window = landed, window
        self.pair_send, self.pair_recv, self.send, self.recv, self.hand_send, self.hand_recv = sems
        self.phases = len(plane.across)
        self.depth, self.half = pair_buf.shape[1:]
        self.shared = window.shape[2] - self.half
        self.place = self.lanes(plane.core * self.shared, self.half)

    def lanes(self, offset, size):
        return pl.ds(pl.multiple_of(offset, 128), size)

    def side(self, which):
        return pl.ds(pl.multiple_of(which * (self.depth // 2), SUB), self.depth // 2)

    def pair(self, r):
        source = self.part.at[r, :, self.lanes((1 - self.plane.core) * self.half, self.half)]
        return remote(source, self.pair_buf.at[r], self.pair_send.at[r], self.pair_recv.at[r], self.plane.partner)

    def hand(self, r):
        core, half, shared = self.plane.core, self.half, self.shared
        source = self.window.at[r, :, self.lanes((1 - core) * (half - shared) + core * shared, shared)]
        target = self.window.at[r, :, self.lanes(core * half, shared)]
        return remote(source, target, self.hand_send.at[r], self.hand_recv.at[r], self.plane.partner)

    def cross(self, r, phase, side):
        device = self.plane.across[(phase + side) % self.phases]
        rows = self.side(side)
        sems = (self.send.at[r, phase, side], self.recv.at[r, phase, side])
        return remote(self.sums.at[r, phase, rows], self.landed.at[r, phase, rows], *sems, device)

    def scatter(self, r, phase, arriving=False):
        keep, away = self.plane.high, 1 - self.plane.high
        sems = (self.send.at[r, phase, 0], self.recv.at[r, phase, 0])
        if phase == 0:
            rows = self.side(keep if arriving else away)
            return remote(self.sums.at[r, 0, rows], self.landed.at[r, 0, rows], *sems, self.plane.across[1])
        if phase == 1:
            rows = self.side(keep)
            return remote(self.sums.at[r, 1, rows], self.landed.at[r, 1, rows], *sems, self.plane.across[0])
        place = self.window.at[r, self.side(away if arriving else keep), self.place]
        return remote(place, place, *sems, self.plane.across[1])

    def begin(self, r):
        self.pair(r).start()

    def steps(self, double):
        return self.phases + 1 if double else 4

    def advance(self, r, phase, double):
        if phase == 0:
            self.pair(r).wait_recv()
            own = self.lanes(self.plane.core * self.half, self.half)
            self.sums[r, 0] = self.part[r, :, own] + self.pair_buf[r]
            if double:
                for side in range(2):
                    self.cross(r, 0, side).start()
            else:
                self.scatter(r, 0).start()
            return
        if double:
            for side in range(2):
                rows = self.side(side)
                self.cross(r, phase - 1, side).wait_recv()
                total = self.sums[r, phase - 1, rows] + self.landed[r, phase - 1, rows]
                if phase < self.phases:
                    self.sums[r, phase, rows] = total
                    self.cross(r, phase, side).start()
                else:
                    self.window[r, rows, self.place] = total
            if phase == self.phases:
                self.hand(r).start()
            return
        self.scatter(r, phase - 1, True).wait_recv()
        if phase == 3:
            self.hand(r).start()
            return
        rows = self.side(self.plane.high)
        total = self.sums[r, phase - 1, rows] + self.landed[r, phase - 1, rows]
        if phase == 1:
            self.sums[r, 1, rows] = total
        else:
            self.window[r, rows, self.place] = total
        self.scatter(r, phase).start()

    def arrive(self, r):
        core, half, shared = self.plane.core, self.half, self.shared
        target = self.window.at[r, :, self.lanes((1 - core) * half, shared)]
        remote(target, target, self.hand_send.at[r], self.hand_recv.at[r], self.plane.partner).wait_recv()

    def drain(self, r, double):
        self.pair(r).wait_send()
        self.hand(r).wait_send()
        if double:
            for phase in range(self.phases):
                for side in range(2):
                    self.cross(r, phase, side).wait_send()
        else:
            for phase in range(3):
                self.scatter(r, phase).wait_send()


def eliminate(rows, finish):
    groups = len(rows)
    wide = rows[0].shape
    index = lax.broadcasted_iota(jnp.int32, wide, 0)
    rows = list(rows)
    for panel in range(groups):
        first = panel * SUB
        cols = {
            q: [jnp.broadcast_to(rows[q][:, first + k : first + k + 1], wide) for k in range(SUB)]
            for q in range(panel, groups)
        }
        own = cols[panel]
        square = jnp.broadcast_to(own[0][0:1], wide)
        for k in range(SUB):
            scale = lax.rsqrt(square)
            if k + 1 < SUB:
                beside = jnp.broadcast_to(own[k][k + 1 : k + 2], wide) * scale
                square = jnp.broadcast_to(own[k + 1][k + 1 : k + 2], wide) - beside * beside
            pivot = jnp.broadcast_to(rows[panel][k : k + 1], wide) * scale
            weight = {q: cols[q][k] * scale for q in range(panel, groups)}
            across = weight[panel]
            below = jnp.where(index > k, across, 0.0)
            rows[panel] = jnp.where(index == k, pivot, rows[panel] - below * pivot)
            for j in range(k + 1, SUB):
                factor = jnp.broadcast_to(across[j : j + 1], wide)
                for q in range(panel, groups):
                    cols[q][j] = cols[q][j] - (below if q == panel else weight[q]) * factor
            for q in range(panel + 1, groups):
                rows[q] = rows[q] - weight[q] * pivot
        finish(panel, rows[panel])
    return rows


def factor(gram, work, upper, send):
    columns = gram.shape[0]
    eye = jnp.where(
        lax.broadcasted_iota(jnp.int32, (columns, columns), 0)
        == lax.broadcasted_iota(jnp.int32, (columns, columns), 1),
        1.0,
        0.0,
    )
    work[:, :columns] = gram
    work[:, columns:] = eye
    diagonal = gram[:NB, :NB]
    for block in range(columns // NB):
        begin, end = block * NB, (block + 1) * NB
        if begin > 0:
            upper[begin:end, :begin] = jnp.zeros((NB, begin), jnp.float32)

        def finish(panel, values):
            start = panel * SUB
            lane = lax.broadcasted_iota(jnp.int32, (SUB, NB), 1)
            row = lax.broadcasted_iota(jnp.int32, (SUB, NB), 0) + start
            upper[begin + start : begin + start + SUB, begin:end] = jnp.where(lane >= row, values[:, :NB], 0.0)
            if end == columns and (start + SUB) % PIECE == 0:
                send((begin + start) // PIECE).start()

        both = jnp.concatenate([diagonal, eye[:NB, :NB]], axis=1)
        done = eliminate([both[q * SUB : (q + 1) * SUB] for q in range(NB // SUB)], finish)
        inverse = jnp.concatenate(done, axis=0)[:, NB:]
        if end < columns:
            right = mm3(inverse, work[begin:end, end:columns])
            rest = work[end:, end:columns] - mm3(right, right, TN)
            diagonal = rest[:NB, :NB]
            work[end:, end:columns] = rest
            upper[begin:end, end:] = right
            for piece in range(begin // PIECE, end // PIECE):
                send(piece).start()
        left = mm3(inverse, work[begin:end, columns:])
        work[begin:end, columns:] = left
        if end < columns:
            work[end:, columns:] = work[end:, columns:] - mm3(right, left, TN)


def whole_kernel(
    bound_ref, pattern_hbm, omega_ref, contrib_ref, assembled_ref, maps_hbm, bases_ref, coupling_ref,
    pattern_ref, maps_ref, gathered, contrib_buf, assembled_buf, pick, place, front, entries,
    part, sums, pair_buf, landed, window, work, upper, sibling, bases_out, bases_in, coupling_out, coupling_in,
    bases_buf, input_sems, *sems,
):
    plane = Plane()
    core = plane.core
    window_rows = assembled_buf.shape[1]
    columns, width = upper.shape[1], bases_buf.shape[0]
    stages, span = window.shape[0], window.shape[2]
    low = window_rows - span
    held = (pick, place, front, entries)
    load_front = pltpu.make_async_copy(contrib_ref.at[0], contrib_buf, input_sems.at[0])
    load_entries = pltpu.make_async_copy(assembled_ref.at[0], assembled_buf, input_sems.at[1])
    load_small = [
        pltpu.make_async_copy(source, target, input_sems.at[2 + i])
        for i, (source, target) in enumerate(
            ((maps_hbm, maps_ref), (pattern_hbm, pattern_ref))
        )
    ]
    for copy in load_small + [load_front, load_entries]:
        copy.start()
    greet(plane)

    row_count, row_pos = lax.axis_size("row"), lax.axis_index("row")
    gather = Gather(omega_ref, gathered, sems[:8])
    summing = Total(plane, part, sums, pair_buf, landed, window, sems[8:14])

    def prepare():
        for copy in load_small + [load_front, load_entries]:
            copy.wait()
        prepare_sketch(pattern_ref, contrib_buf, assembled_buf, maps_ref, held)

    def block_of(n):
        return row_pos if n == 0 else gather.nth(n)

    def double(n):
        return n >= stages - DOUBLED

    def stage(n):
        block = block_of(n)
        if n > 0:
            gather.arrive(block)
        sketch(gathered[block].reshape(columns // stages, window_rows), held, part.at[block])
        summing.begin(block)

    if stages == row_count:
        begun, left = [], {}

        def begin(n):
            stage(n)
            begun.append(n)
            left[n] = list(range(summing.steps(double(n))))

        def go(n):
            if n in left and left[n]:
                summing.advance(block_of(n), left[n].pop(0), double(n))

        def go_all():
            for n in list(begun):
                go(n)

        end, mid = gather.chunks - 1, gather.chunks // 2
        queue = {(0, end): [prepare, lambda: begin(0)]}
        for step, chunk, n in EARLY:
            if step < row_count:
                queue.setdefault((step, min(chunk, end)), []).append(
                    (lambda n=n: begin(n - 10)) if n >= 10 else (lambda n=n: go(n))
                )
        gather.run(queue)
        for n in LATE:
            if n >= 10 and 10 + len(begun) <= n < 10 + stages:
                begin(n - 10)
            elif n < 10:
                go(n)
        for n in range(len(begun), stages):
            begin(n)
            go_all()
        while any(left.values()):
            go_all()
        blocks = range(stages)
        landing = [block_of(n) for n in blocks]
    else:
        gather.run({(0, 0): [prepare]})
        for step in range(1, row_count):
            gather.arrive(lax.rem(row_pos + step, row_count))
        sketch(gathered[...].reshape(columns, window_rows), held, part.at[0])
        summing.begin(0)
        for phase in range(summing.steps(True)):
            summing.advance(0, phase, True)
        blocks, landing = [], [0]

    near_send, near_recv, end_send, end_recv = sems[14:]
    near = {"row": row_pos + 1 - 2 * (row_pos % 2)}

    def send(piece):
        start = piece * PIECE // 128 * 128
        rows = slice(piece * PIECE, (piece + 1) * PIECE)
        source, target = upper.at[rows, start:], sibling.at[rows, start:]
        return remote(source, target, near_send.at[piece], near_recv.at[piece], near)

    bound = bound_ref[...]
    rows_of_leaf = (1 - core) * bound + core * (window_rows - bound)

    def leaf_gram(lanes, first):
        values = window[:, :, lanes].reshape(columns, lanes.size)
        place_of = lax.broadcasted_iota(jnp.int32, values.shape, 1) + first
        masked = jnp.where((1 - 2 * core) * (bound - place_of) + core > 0, values, 0.0)
        return mm3(masked, masked, NT)

    half, shared = summing.half, summing.shared
    gram = leaf_gram(summing.place, core * half)
    for block in landing:
        summing.arrive(block)
    gram = gram + leaf_gram(summing.lanes((1 - core) * half, shared), core * low + (1 - core) * half)
    factor(gram / rows_of_leaf.astype(jnp.float32), work, upper, send)
    samples = window[...].reshape(columns, span)

    pair_rows = pl.ds(pl.multiple_of(plane.chip * 2 * width, 2 * width), 2 * width)
    give_bases = remote(
        bases_out.at[1 - core], bases_in.at[core], end_send.at[0], end_recv.at[0], plane.partner
    )
    give_coupling = remote(
        coupling_out.at[1 - core], coupling_in.at[core], end_send.at[1], end_recv.at[1], plane.partner
    )
    bases_out[...] = mm3(work[pair_rows, columns:], samples).reshape(bases_out.shape)
    give_bases.start()
    bases_in[core] = bases_out[core]
    own = upper[pair_rows, :]
    finished = []

    def finish(source, target):
        copy = pltpu.make_async_copy(source, target, input_sems.at[len(finished)])
        copy.start()
        finished.append(copy)

    pieces = columns // PIECE
    for piece in range(pieces):
        if piece == pieces // 2:
            remote(
                bases_out.at[core], bases_in.at[1 - core], end_send.at[0], end_recv.at[0], plane.partner
            ).wait_recv()
            bases_buf[:, :low] = bases_in[0, :, :low]
            bases_buf[:, span:] = bases_in[1, :, span - low :]
            lane = lax.broadcasted_iota(jnp.int32, (width, span - low), 1) + low
            bases_buf[:, low:span] = jnp.where(lane < bound, bases_in[0, :, low:], bases_in[1, :, : span - low])
            finish(bases_buf, bases_ref)
        start = piece * PIECE // 128 * 128
        rows = slice(piece * PIECE, (piece + 1) * PIECE)
        send(piece).wait_recv()
        product = mm3(own[:, start:], sibling[rows, start:], NT)
        coupling_out[:, :, rows] = product.reshape(2, width, PIECE)
    give_coupling.start()
    finish(coupling_out.at[core], coupling_ref.at[0, core])
    remote(
        coupling_out.at[core], coupling_in.at[1 - core], end_send.at[1], end_recv.at[1], plane.partner
    ).wait_recv()
    finish(coupling_in.at[1 - core], coupling_ref.at[0, 1 - core])

    gather.drain()
    for n in blocks:
        summing.drain(block_of(n), double(n))
    if not blocks:
        summing.drain(0, True)
    for piece in range(columns // PIECE):
        send(piece).wait_send()
    give_bases.wait_send()
    give_coupling.wait_send()
    for copy in finished:
        copy.wait()


def deliver_kernel(bases_ref, coupling_ref, bases_out, coupling_out):
    bases_out[...] = bases_ref[...]
    coupling_out[...] = coupling_ref[...]


def local(contrib, assembled, pattern, omega, row_maps, leaf_bounds):
    tile_rows, tile_cols = contrib.shape[1:]
    window_rows, own_width = omega.shape
    rows = lax.axis_size("row")
    cols = lax.axis_size("col")
    chips = cols * lax.axis_size("child") // 2
    columns = own_width * rows
    width = columns // (2 * chips)
    phases = 1 + (cols // 2).bit_length() - 1
    span = (window_rows // 2 + window_rows // 16 + 127) // 128 * 128
    own = omega.T.reshape(2, own_width // 2, window_rows)
    f32, bf16, dma = jnp.float32, jnp.bfloat16, pltpu.SemaphoreType.DMA
    any_space = pl.BlockSpec(memory_space=pl.ANY)
    stages = rows if own_width >= 8 * SUB else 1
    depth = columns // stages
    chunks = own_width // 2 // CHUNK
    bases, coupling = pl.pallas_call(
        whole_kernel,
        out_shape=(
            jax.ShapeDtypeStruct((width, window_rows), f32),
            jax.ShapeDtypeStruct((1, 2, width, columns), f32),
        ),
        in_specs=[VMEM] + [any_space] * 5,
        out_specs=(any_space, any_space),
        scratch_shapes=[
            pltpu.SMEM(pattern.shape, jnp.int32),
            pltpu.VMEM(row_maps.shape, jnp.int32),
            pltpu.VMEM((rows, 2, own_width // 2, window_rows), f32),
            pltpu.VMEM((tile_rows, tile_cols), f32),
            pltpu.VMEM((tile_rows, window_rows), f32),
            pltpu.VMEM((window_rows, tile_cols), bf16),
            pltpu.VMEM((window_rows, tile_rows), bf16),
            pltpu.VMEM((2, tile_rows, tile_cols), bf16),
            pltpu.VMEM((2, tile_rows, window_rows), bf16),
            pltpu.VMEM((stages, depth, window_rows), f32),
            pltpu.VMEM((stages, phases, depth, window_rows // 2), f32),
            pltpu.VMEM((stages, depth, window_rows // 2), f32),
            pltpu.VMEM((stages, phases, depth, window_rows // 2), f32),
            pltpu.VMEM((stages, depth, span), f32),
            pltpu.VMEM((columns, 2 * columns), f32),
            pltpu.VMEM((columns, columns), f32),
            pltpu.VMEM((columns, columns), f32),
            pltpu.VMEM((2, width, span), f32),
            pltpu.VMEM((2, width, span), f32),
            pltpu.VMEM((2, width, columns), f32),
            pltpu.VMEM((2, width, columns), f32),
            pltpu.VMEM((width, window_rows), f32),
            dma((4,)),
        ]
        + [dma((rows, chunks))] * 7
        + [dma]
        + [dma((stages,))] * 2
        + [dma((stages, max(phases, 3), 2))] * 2
        + [dma((stages,))] * 2
        + [dma((columns // PIECE,))] * 2
        + [dma((2,))] * 2,
        compiler_params=pltpu.CompilerParams(
            collective_id=0, has_side_effects=True, vmem_limit_bytes=(64 << 20) - ROOM
        ),
        name="front_samples",
    )(leaf_bounds.reshape(1, 1), pattern, own, contrib, assembled, row_maps)
    bases, coupling = pl.pallas_call(
        deliver_kernel,
        out_shape=(
            jax.ShapeDtypeStruct(bases.shape, f32),
            jax.ShapeDtypeStruct(coupling.shape, f32),
        ),
        in_specs=[VMEM, VMEM],
        out_specs=(VMEM, VMEM),
        compiler_params=pltpu.CompilerParams(vmem_limit_bytes=SMALL),
        name="deliver",
    )(bases, coupling)
    return (bases.T, coupling)


def solution(mesh):
    in_specs = (
        P("child", "row", "col"),
        P("child", "row", "col"),
        P("row", "col"),
        P("col", "row"),
        P("child", None),
        P("row"),
    )
    out_specs = (P("row", ("child", "col")), P("row", None, ("child", "col"), None))
    return jax.shard_map(local, mesh=mesh, in_specs=in_specs, out_specs=out_specs, check_vma=False)
```
